256 devices in a mesh: ctx: 32 (over x, y, core), head: 8 (over z).
Axes of the slice: x: 4, y: 4, z: 8, core: 2. Of those that a mesh axis runs over, the one named last changes fastest.
Arguments:
- queries: bfloat16 [32768, 4096], P(('ctx', 'head')), may hold values from -6 to 6
- keys: bfloat16 [32768, 4096], P(('ctx', 'head')), may hold values from -6 to 6
- values: bfloat16 [32768, 4096], P(('ctx', 'head')), may hold values from -6 to 6
- out_grad: bfloat16 [32768, 4096], P(('ctx', 'head')), may hold values from -1024 to 1024, as said below
Outputs:
- grad_queries: bfloat16 [32768, 4096], P(('ctx', 'head'))
- grad_keys: bfloat16 [32768, 4096], P(('ctx', 'head'))
- grad_values: bfloat16 [32768, 4096], P(('ctx', 'head'))
The draws below stay inside these ranges and needn't reach their ends.
Inputs may be any that keep to these rules, and one draw needn't show every extreme that they name: `out_grad`: output gradients of varying size along the sequence.
All inputs are finite; a program needn't handle non-finite values.
Results may differ from the reference program's by a relative error of at most 0.011.
Values may be sent and summed in bfloat16 or wider, within the bound.
No kernel may reach another device: no remote copies, remote signals or barrier semaphores. Data moves between devices by JAX's collectives and lax.ppermute only.
A program may use at most 128 MiB of HBM per device.

```python
import jax
import jax.numpy as jnp
from jax import lax

HEADS = 32
HD = 128
BLOCK = 512
SEQ = 32768


def draw_out_grad(key, part):
    noise = jnp.clip(jax.random.normal(key, (SEQ, HEADS * HD), jnp.float32), -4.0, 4.0)
    rising = 2.0 * jnp.sqrt(jnp.arange(SEQ, dtype=jnp.float32) + 1.0)
    return jnp.clip(noise * rising[:, None], -1024.0, 1024.0).astype(jnp.bfloat16)


def shard_levels(key, dims, split, least, top_value):
    gain = 1.0
    for position, shards_of in split:
        draws = jax.random.uniform(jax.random.fold_in(jax.random.fold_in(key, 6), position), (shards_of,), jnp.float32, least / len(split), top_value / len(split))
        gain = gain * jnp.repeat(jnp.exp(draws), dims[position] // shards_of).reshape((-1,) + (1,) * (len(dims) - 1 - position))
    return gain


def bell_draw(stream_key, shape, width, reach, pieces=(), kind=jnp.bfloat16):
    level = shard_levels(stream_key, shape, pieces, -0.22, 0.18) if pieces else 1.0
    array = jax.random.normal(stream_key, shape, jnp.float32) * width * level
    return jnp.minimum(jnp.maximum(array, -reach), reach).astype(kind)


def setup_inputs(seed: int = 0) -> dict:
    key_list = jax.random.split(jax.random.key(seed), 5)
    queries = bell_draw(key_list[0], (SEQ, HEADS * HD), 1.0, 6.0, ((0, 256),))
    keys = bell_draw(key_list[1], (SEQ, HEADS * HD), 1.0, 6.0, ((0, 256),))
    values = bell_draw(key_list[2], (SEQ, HEADS * HD), 1.0, 6.0, ((0, 256),))
    out_grad = draw_out_grad(jax.random.fold_in(key_list[4], 71), 0)
    return dict(queries=queries, keys=keys, values=values, out_grad=out_grad)


def feature(inputs):
    real = inputs.astype(jnp.float32)
    return jnp.where(real > 0, real + 1.0, jnp.exp(jnp.minimum(real, 0.0)))


def slope(inputs):
    real = inputs.astype(jnp.float32)
    return jnp.where(real > 0, 1.0, jnp.exp(jnp.minimum(real, 0.0)))


def forward_block(query_feat, key_feat, value_rows, grad_rows, prefix_state, prefix_sum):
    length = query_feat.shape[0]
    causal = jnp.arange(length)[:, None] >= jnp.arange(length)[None, :]
    scores = jnp.where(causal, jnp.dot(query_feat, key_feat.T, preferred_element_type=jnp.float32), 0.0)
    weights = scores.astype(jnp.bfloat16)
    state_half = prefix_state.astype(jnp.bfloat16)
    numerator = jnp.dot(weights, value_rows, preferred_element_type=jnp.float32) + jnp.dot(query_feat, state_half, preferred_element_type=jnp.float32)
    denominator = jnp.sum(scores, axis=1) + jnp.dot(query_feat.astype(jnp.float32), prefix_sum, precision=lax.Precision.HIGHEST)
    attended = numerator / denominator[:, None]
    grad_real = grad_rows.astype(jnp.float32)
    grad_numerator = (grad_real / denominator[:, None]).astype(jnp.bfloat16)
    grad_denominator = -jnp.sum(grad_real * attended, axis=1) / denominator
    mixing = jnp.where(causal, jnp.dot(grad_numerator, value_rows.T, preferred_element_type=jnp.float32) + grad_denominator[:, None], 0.0).astype(jnp.bfloat16)
    grad_query_feat = jnp.dot(mixing, key_feat, preferred_element_type=jnp.float32) + jnp.dot(grad_numerator, state_half.T, preferred_element_type=jnp.float32) + grad_denominator[:, None] * prefix_sum[None, :]
    return grad_query_feat, grad_numerator, grad_denominator


def backward_block(query_feat, key_feat, value_rows, grad_numerator, grad_denominator, suffix_state, suffix_sum):
    length = query_feat.shape[0]
    causal = jnp.arange(length)[:, None] >= jnp.arange(length)[None, :]
    scores = jnp.where(causal, jnp.dot(query_feat, key_feat.T, preferred_element_type=jnp.float32), 0.0)
    weights = scores.astype(jnp.bfloat16)
    mixing = jnp.where(causal, jnp.dot(grad_numerator, value_rows.T, preferred_element_type=jnp.float32) + grad_denominator[:, None], 0.0).astype(jnp.bfloat16)
    state_half = suffix_state.astype(jnp.bfloat16)
    grad_key_feat = jnp.dot(mixing.T, query_feat, preferred_element_type=jnp.float32) + jnp.dot(value_rows, state_half.T, preferred_element_type=jnp.float32) + suffix_sum[None, :]
    grad_value = jnp.dot(weights.T, grad_numerator, preferred_element_type=jnp.float32) + jnp.dot(key_feat, state_half, preferred_element_type=jnp.float32)
    return grad_key_feat, grad_value.astype(jnp.bfloat16)


def per_head(inputs):
    query_rows, key_rows, value_rows, grad_rows = inputs
    query_feat = feature(query_rows).astype(jnp.bfloat16)
    key_feat = feature(key_rows).astype(jnp.bfloat16)

    def forward_step(carry, blocks):
        prefix_state, prefix_sum = carry
        query_blk, key_blk, value_blk, grad_blk = blocks
        outputs = forward_block(query_blk, key_blk, value_blk, grad_blk, prefix_state, prefix_sum)
        update = jnp.dot(key_blk.T, value_blk, preferred_element_type=jnp.float32)
        key_total = jnp.sum(key_blk.astype(jnp.float32), axis=0)
        return (prefix_state + update, prefix_sum + key_total), outputs

    start_state = (jnp.zeros((HD, HD), jnp.float32), jnp.zeros((HD,), jnp.float32))
    ignored, forward_out = lax.scan(forward_step, start_state, (query_feat, key_feat, value_rows, grad_rows))
    grad_query_feat, grad_numerator, grad_denominator = forward_out

    def backward_step(carry, blocks):
        suffix_state, suffix_sum = carry
        query_blk, key_blk, value_blk, numer_blk, denom_blk = blocks
        outputs = backward_block(query_blk, key_blk, value_blk, numer_blk, denom_blk, suffix_state, suffix_sum)
        update = jnp.dot(query_blk.T, numer_blk, preferred_element_type=jnp.float32)
        query_total = jnp.sum(denom_blk[:, None] * query_blk.astype(jnp.float32), axis=0)
        return (suffix_state + update, suffix_sum + query_total), outputs

    ignored, backward_out = lax.scan(backward_step, start_state, (query_feat, key_feat, value_rows, grad_numerator, grad_denominator), reverse=True)
    grad_key_feat, grad_value = backward_out
    grad_query = (grad_query_feat * slope(query_rows)).astype(jnp.bfloat16)
    grad_key = (grad_key_feat * slope(key_rows)).astype(jnp.bfloat16)
    return grad_query, grad_key, grad_value


def reference(queries, keys, values, out_grad):
    def heads_first(inputs):
        return inputs.reshape(SEQ // BLOCK, BLOCK, HEADS, HD).transpose(2, 0, 1, 3)

    def tokens_first(inputs):
        return inputs.transpose(1, 2, 0, 3).reshape(SEQ, HEADS * HD)

    results = lax.map(per_head, (heads_first(queries), heads_first(keys), heads_first(values), heads_first(out_grad)))
    return tokens_first(results[0]), tokens_first(results[1]), tokens_first(results[2])
```

```python
import functools

import jax
import jax.numpy as jnp
from jax import lax
from jax.experimental import pallas as pl
from jax.experimental.pallas import tpu as pltpu
from jax.sharding import PartitionSpec as P

HD = 128

F32 = jnp.float32
BF16 = jnp.bfloat16


def feature(real):
    return jnp.where(real > 0, real + 1.0, jnp.exp(jnp.minimum(real, 0.0)))


def slope(real):
    return jnp.where(real > 0, 1.0, jnp.exp(jnp.minimum(real, 0.0)))


def dot_nn(a, b):
    return lax.dot_general(a, b, (((1,), (0,)), ((), ())), preferred_element_type=F32)


def dot_nt(a, b):
    return lax.dot_general(a, b, (((1,), (1,)), ((), ())), preferred_element_type=F32)


def dot_tn(a, b):
    return lax.dot_general(a, b, (((0,), (0,)), ((), ())), preferred_element_type=F32)


def causal(n):
    return lax.broadcasted_iota(jnp.int32, (n, n), 0) >= lax.broadcasted_iota(jnp.int32, (n, n), 1)


def columns(j):
    return slice(j * HD, (j + 1) * HD)


def head_row(ref, step, j):
    return ref[pl.ds(pl.program_id(0) * step + j, 1), :]


def put_head_row(ref, step, j, row):
    ref[pl.ds(pl.program_id(0) * step + j, 1), :] = row


def each(fn, *lists):
    return [fn(*items) for items in zip(*lists)]


def key_state_kernel(step, k_ref, v_ref, state_ref, sum_ref):
    heads = range(step)
    fk = [feature(k_ref[:, columns(j)].astype(F32)).astype(BF16) for j in heads]
    states = [dot_tn(fk[j], v_ref[:, columns(j)]) for j in heads]
    for j in heads:
        put_head_row(sum_ref, step, j, jnp.sum(fk[j].astype(F32), axis=0, keepdims=True))
    for j in heads:
        state_ref[j] = states[j].astype(BF16)


def scores_of(fq, fk, zrows, mask):
    scores = [jnp.where(mask, s, 0.0) for s in each(dot_nt, fq, fk)]
    dens = [
        jnp.sum(s + f.astype(F32) * zrow, axis=1, keepdims=True)
        for s, f, zrow in zip(scores, fq, zrows)
    ]
    return [s.astype(BF16) for s in scores], [1.0 / den for den in dens]


def query_state_kernel(step, q_ref, k_ref, g_ref, z_ref, state_ref):
    mask = causal(q_ref.shape[0])
    heads = range(step)
    fq = [feature(q_ref[:, columns(j)].astype(F32)).astype(BF16) for j in heads]
    fk = [feature(k_ref[:, columns(j)].astype(F32)).astype(BF16) for j in heads]
    _, inverse = scores_of(fq, fk, [head_row(z_ref, step, j) for j in heads], mask)
    dnum = [(g_ref[:, columns(j)].astype(F32) * inverse[j]).astype(BF16) for j in heads]
    states = each(dot_tn, fq, dnum)
    for j in heads:
        state_ref[j] = states[j].astype(BF16)


def query_grad_kernel(step, q_ref, k_ref, v_ref, g_ref, z_ref, s_ref, gq_ref, dfk_ref, gv_ref, sum_ref):
    mask = causal(q_ref.shape[0])
    heads = range(step)
    fq32 = [feature(q_ref[:, columns(j)].astype(F32)) for j in heads]
    fq = [f.astype(BF16) for f in fq32]
    fk = [feature(k_ref[:, columns(j)].astype(F32)).astype(BF16) for j in heads]
    zrows = [head_row(z_ref, step, j) for j in heads]
    v = [v_ref[:, columns(j)] for j in heads]
    weights, inverse = scores_of(fq, fk, zrows, mask)
    num = [dot_nn(weights[j], v[j]) + dot_nn(fq[j], s_ref[j]) for j in heads]
    dnum = [(g_ref[:, columns(j)].astype(F32) * inverse[j]).astype(BF16) for j in heads]
    pair = each(dot_nt, dnum, v)
    shared = [
        jnp.sum(g_ref[:, columns(j)].astype(F32) * num[j], axis=1, keepdims=True) for j in heads
    ]
    dden = [-(s * i) * i for s, i in zip(shared, inverse)]
    mixing = [jnp.where(mask, p + d, 0.0).astype(BF16) for p, d in zip(pair, dden)]
    for j in heads:
        gv_ref[:, columns(j)] = dot_tn(weights[j], dnum[j])
    for j in heads:
        put_head_row(sum_ref, step, j, jnp.sum(dden[j] * fq[j].astype(F32), axis=0, keepdims=True))
    dfq = [
        dot_nn(mixing[j], fk[j]) + dot_nt(dnum[j], s_ref[j]) + dden[j] * zrows[j] for j in heads
    ]
    for j in heads:
        gq_ref[:, columns(j)] = (dfq[j] * jnp.minimum(fq32[j], 1.0)).astype(BF16)
    for j in heads:
        dfk_ref[:, columns(j)] = dot_tn(mixing[j], fq[j])


def key_grad_kernel(step, k_ref, v_ref, dfk_ref, gv_ref, rs_ref, dfk_out_ref, gv_out_ref):
    heads = range(step)
    fk = [feature(k_ref[:, columns(j)].astype(F32)).astype(BF16) for j in heads]
    for j in heads:
        c = columns(j)
        dfk_out_ref[:, c] = dfk_ref[:, c] + dot_nt(v_ref[:, c], rs_ref[j])
    for j in heads:
        c = columns(j)
        gv_out_ref[:, c] = (gv_ref[:, c] + dot_nn(fk[j], rs_ref[j])).astype(BF16)


def key_finish_kernel(step, k_ref, dfk_ref, rz_ref, gk_ref):
    for j in range(step):
        c = columns(j)
        dfk = dfk_ref[:, c] + head_row(rz_ref, step, j)
        gk_ref[:, c] = (dfk * slope(k_ref[:, c].astype(F32))).astype(BF16)


def head_call(kernel, step, kinds_in, kinds_out, arrays, tokens, heads):
    wide = pl.BlockSpec((tokens, step * HD), lambda i: (0, i))
    square = pl.BlockSpec((step, HD, HD), lambda i: (i, 0, 0))
    rows = pl.BlockSpec((heads, HD), lambda i: (0, 0))
    specs = {"w": wide, "f": wide, "s": square, "r": rows}
    shapes = {
        "w": jax.ShapeDtypeStruct((tokens, heads * HD), BF16),
        "f": jax.ShapeDtypeStruct((tokens, heads * HD), F32),
        "s": jax.ShapeDtypeStruct((heads, HD, HD), BF16),
        "r": jax.ShapeDtypeStruct((heads, HD), F32),
    }
    return pl.pallas_call(
        functools.partial(kernel, step),
        grid=(heads // step,),
        in_specs=[specs[t] for t in kinds_in],
        out_specs=[specs[t] for t in kinds_out],
        out_shape=[shapes[t] for t in kinds_out],
        compiler_params=pltpu.CompilerParams(dimension_semantics=("arbitrary",)),
    )(*arrays)


def z_total_kernel(x_ref, tot_ref):
    tot = x_ref[0].astype(F32)
    for z in range(1, x_ref.shape[0]):
        tot = tot + x_ref[z].astype(F32)
    tot_ref[...] = tot


def z_running_kernel(forward, x_ref, base_ref, out_ref):
    n = x_ref.shape[0]
    acc = base_ref[...]
    for s in range(n):
        z = s if forward else n - 1 - s
        out_ref[z] = acc.astype(BF16)
        if s < n - 1:
            acc = acc + x_ref[z].astype(F32)


def z_total(x):
    n, rows, lanes = x.shape
    return pl.pallas_call(
        z_total_kernel,
        grid=(1,),
        in_specs=[pl.BlockSpec((n, rows, lanes), lambda i: (0, i, 0))],
        out_specs=pl.BlockSpec((rows, lanes), lambda i: (i, 0)),
        out_shape=jax.ShapeDtypeStruct((rows, lanes), F32),
    )(x)


def z_running(x, base, forward):
    n, rows, lanes = x.shape
    return pl.pallas_call(
        functools.partial(z_running_kernel, forward),
        grid=(1,),
        in_specs=[
            pl.BlockSpec((n, rows, lanes), lambda i: (0, i, 0)),
            pl.BlockSpec((rows, lanes), lambda i: (i, 0)),
        ],
        out_specs=pl.BlockSpec((n, rows, lanes), lambda i: (0, i, 0)),
        out_shape=jax.ShapeDtypeStruct((n, rows, lanes), BF16),
    )(x, base)


def level(part, total, n, place, hop, forward, wire):
    before = None
    d = 1
    while d < n:
        if total is None:
            got_part, got_total = hop(part.astype(wire), d).astype(F32), None
        elif total is part:
            got_part = got_total = hop(part.astype(wire), d).astype(F32)
        else:
            got = hop(jnp.stack([part, total]).astype(wire), d).astype(F32)
            got_part, got_total = got[0], got[1]
        ok = (place >= d) if forward else (place < n - d)
        masked = jnp.where(ok, got_part, 0.0)
        before = masked if before is None else before + masked
        part, total = part + masked, None if total is None else total + got_total
        d *= 2
    return before, total


def grid_of(ctx):
    side = 1
    while side * side * 2 < ctx:
        side += 1
    return side


def ctx_hop(side, which, forward):
    def hop(value, d):
        d = d if forward else -d
        pairs = []
        for x in range(side):
            for y in range(side):
                for c in range(2):
                    to = (x, (y + d) % side) if which == "y" else ((x + d) % side, y)
                    pairs.append(((x * side + y) * 2 + c, (to[0] * side + to[1]) * 2 + c))
        return lax.ppermute(value, "ctx", pairs)

    return hop


def swap_cores(value, ctx):
    return lax.ppermute(value, "ctx", [(i, i ^ 1) for i in range(ctx)])


def ctx_running(total, ctx, forward, wire, split):
    side = grid_of(ctx)
    place = lax.axis_index("ctx")
    core, y, x = place % 2, (place // 2) % side, place // (2 * side)
    other = swap_cores(total, ctx)
    by_core = jnp.where((core == 1) if forward else (core == 0), other, 0.0)
    chip = total + other
    half = total.shape[0] // 2
    if split:
        chip = jnp.where(core == 0, chip[:half], chip[half:])
    by_y, row = level(chip, chip, side, y, ctx_hop(side, "y", forward), forward, wire)
    by_x, _ = level(row, None, side, x, ctx_hop(side, "x", forward), forward, wire)
    base = by_y + by_x
    if split:
        got = swap_cores(base, ctx)
        base = jnp.concatenate([jnp.where(core == 0, base, got), jnp.where(core == 0, got, base)])
    return by_core + base


def z_gather(x, group):
    return lax.all_to_all(jnp.broadcast_to(x[None], (group, *x.shape)), "head", 0, 0, tiled=True)


def shards(ctx, group, queries, keys, values, out_grad):
    tokens, width = queries.shape
    heads = width // HD
    call = functools.partial(head_call, tokens=tokens, heads=heads)
    owned = heads * HD // group
    place = lax.axis_index("head")

    def to_owners(state):
        return lax.all_to_all(state.reshape(group, owned, HD), "head", 0, 0, tiled=True)

    def from_owners(x):
        return lax.all_to_all(x, "head", 0, 0, tiled=True).reshape(heads, HD, HD)

    ranks = jnp.arange(group)[:, None, None]
    key_state, key_sum = call(key_state_kernel, 16, "ww", "sr", (keys, values))
    sums = z_gather(key_sum, group)
    before = jnp.sum(jnp.where(ranks < place, sums, 0.0), axis=0)
    key_state, before, total = lax.optimization_barrier((key_state, before, jnp.sum(sums, axis=0)))
    key_parts = to_owners(key_state)
    z = before + ctx_running(total, ctx, True, F32, False)
    (query_state,) = call(query_state_kernel, 16, "wwwr", "s", (queries, keys, out_grad, z))
    key_parts, query_state = lax.optimization_barrier((key_parts, query_state))
    query_parts = to_owners(query_state)
    key_total = z_total(key_parts)
    key_base = ctx_running(key_total, ctx, True, BF16, True)
    key_running = z_running(key_parts, key_base, True)
    query_parts, key_running = lax.optimization_barrier((query_parts, key_running))
    prefix = from_owners(key_running)
    query_total = z_total(query_parts)
    query_base = ctx_running(query_total, ctx, False, BF16, True)
    query_running = z_running(query_parts, query_base, False)
    prefix, query_running = lax.optimization_barrier((prefix, query_running))
    suffix = from_owners(query_running)
    grad_queries, dfk, gv, query_sum = call(
        query_grad_kernel, 8, "wwwwrs", "wffr", (queries, keys, values, out_grad, z, prefix)
    )
    later = ctx_running(query_sum, ctx, False, F32, False)
    suffix, both = lax.optimization_barrier((suffix, jnp.stack([query_sum, later])))
    sums = z_gather(both, group)
    dfk, grad_values = call(key_grad_kernel, 16, "wwffs", "fw", (keys, values, dfk, gv, suffix))
    r = jnp.sum(sums[:, 1], axis=0) + jnp.sum(jnp.where(ranks > place, sums[:, 0], 0.0), axis=0)
    (grad_keys,) = call(key_finish_kernel, 16, "wfr", "w", (keys, dfk, r))
    return grad_queries, grad_keys, grad_values


def solution(mesh):
    spec = P(("ctx", "head"), None)
    body = functools.partial(shards, mesh.shape["ctx"], mesh.shape["head"])

    return jax.shard_map(
        body, mesh=mesh, in_specs=(spec,) * 4, out_specs=(spec,) * 3, check_vma=False
    )
```

```python
import functools

import jax
import jax.numpy as jnp
from jax import lax
from jax.experimental import pallas as pl
from jax.experimental.pallas import tpu as pltpu
from jax.sharding import PartitionSpec as P

HD = 128

F32 = jnp.float32
BF16 = jnp.bfloat16


def feature(real):
    return jnp.where(real > 0, real + 1.0, jnp.exp(jnp.minimum(real, 0.0)))


def dot_nn(a, b):
    return lax.dot_general(a, b, (((1,), (0,)), ((), ())), preferred_element_type=F32)


def dot_nt(a, b):
    return lax.dot_general(a, b, (((1,), (1,)), ((), ())), preferred_element_type=F32)


def dot_tn(a, b):
    return lax.dot_general(a, b, (((0,), (0,)), ((), ())), preferred_element_type=F32)


def causal(n):
    return lax.broadcasted_iota(jnp.int32, (n, n), 0) >= lax.broadcasted_iota(jnp.int32, (n, n), 1)


def columns(j):
    return slice(j * HD, (j + 1) * HD)


def head_row(ref, step, j):
    return ref[pl.ds(pl.program_id(0) * step + j, 1), :]


def put_head_row(ref, step, j, row):
    ref[pl.ds(pl.program_id(0) * step + j, 1), :] = row


def each(fn, *lists):
    return [fn(*items) for items in zip(*lists)]


def key_state_kernel(step, k_ref, v_ref, state_ref, sum_ref):
    heads = range(step)
    fk = [feature(k_ref[:, columns(j)].astype(F32)).astype(BF16) for j in heads]
    states = [dot_tn(fk[j], v_ref[:, columns(j)]) for j in heads]
    for j in heads:
        put_head_row(sum_ref, step, j, jnp.sum(fk[j].astype(F32), axis=0, keepdims=True))
    for j in heads:
        state_ref[j] = states[j].astype(BF16)


def scores_of(fq, fk, zrows, mask):
    scores = [jnp.where(mask, s, 0.0) for s in each(dot_nt, fq, fk)]
    dens = [
        jnp.sum(s + f.astype(F32) * zrow, axis=1, keepdims=True)
        for s, f, zrow in zip(scores, fq, zrows)
    ]
    return [s.astype(BF16) for s in scores], [1.0 / den for den in dens]


def query_state_kernel(step, q_ref, k_ref, g_ref, z_ref, state_ref):
    mask = causal(q_ref.shape[0])
    heads = range(step)
    fq = [feature(q_ref[:, columns(j)].astype(F32)).astype(BF16) for j in heads]
    fk = [feature(k_ref[:, columns(j)].astype(F32)).astype(BF16) for j in heads]
    _, inverse = scores_of(fq, fk, [head_row(z_ref, step, j) for j in heads], mask)
    dnum = [(g_ref[:, columns(j)].astype(F32) * inverse[j]).astype(BF16) for j in heads]
    states = each(dot_tn, fq, dnum)
    for j in heads:
        state_ref[j] = states[j].astype(BF16)


def num_of(fq, weights, v, s_ref):
    return [dot_nn(w, x) + dot_nn(f, s_ref[j]) for j, (f, w, x) in enumerate(zip(fq, weights, v))]


def dden_of(g_ref, num, inverse):
    shared = [
        jnp.sum(g_ref[:, columns(j)].astype(F32) * n, axis=1, keepdims=True)
        for j, n in enumerate(num)
    ]
    return [-(s * i) * i for s, i in zip(shared, inverse)]


def query_sum_kernel(step, q_ref, k_ref, v_ref, g_ref, z_ref, s_ref, sum_ref):
    mask = causal(q_ref.shape[0])
    heads = range(step)
    fq = [feature(q_ref[:, columns(j)].astype(F32)).astype(BF16) for j in heads]
    fk = [feature(k_ref[:, columns(j)].astype(F32)).astype(BF16) for j in heads]
    weights, inverse = scores_of(fq, fk, [head_row(z_ref, step, j) for j in heads], mask)
    num = num_of(fq, weights, [v_ref[:, columns(j)] for j in heads], s_ref)
    dden = dden_of(g_ref, num, inverse)
    for j in heads:
        row = jnp.sum(dden[j] * fq[j].astype(F32), axis=0, keepdims=True)
        put_head_row(sum_ref, step, j, row)


def query_grad_kernel(step, q_ref, k_ref, v_ref, g_ref, z_ref, s_ref, gq_ref, dfk_ref, gv_ref):
    mask = causal(q_ref.shape[0])
    heads = range(step)
    fq32 = [feature(q_ref[:, columns(j)].astype(F32)) for j in heads]
    fq = [f.astype(BF16) for f in fq32]
    fk = [feature(k_ref[:, columns(j)].astype(F32)).astype(BF16) for j in heads]
    zrows = [head_row(z_ref, step, j) for j in heads]
    v = [v_ref[:, columns(j)] for j in heads]
    weights, inverse = scores_of(fq, fk, zrows, mask)
    num = num_of(fq, weights, v, s_ref)
    dnum = [(g_ref[:, columns(j)].astype(F32) * inverse[j]).astype(BF16) for j in heads]
    pair = each(dot_nt, dnum, v)
    dden = dden_of(g_ref, num, inverse)
    mixing = [jnp.where(mask, p + d, 0.0).astype(BF16) for p, d in zip(pair, dden)]
    for j in heads:
        gv_ref[:, columns(j)] = dot_tn(weights[j], dnum[j])
    dfq = [
        dot_nn(mixing[j], fk[j]) + dot_nt(dnum[j], s_ref[j]) + dden[j] * zrows[j] for j in heads
    ]
    for j in heads:
        gq_ref[:, columns(j)] = (dfq[j] * jnp.minimum(fq32[j], 1.0)).astype(BF16)
    for j in heads:
        dfk_ref[:, columns(j)] = dot_tn(mixing[j], fq[j])


def key_grad_kernel(step, k_ref, v_ref, dfk_ref, gv_ref, rs_ref, rz_ref, gk_ref, gv_out_ref):
    heads = range(step)
    fk32 = [feature(k_ref[:, columns(j)].astype(F32)) for j in heads]
    dfk = [dot_nt(v_ref[:, columns(j)], rs_ref[j]) for j in heads]
    gv = [dot_nn(fk32[j].astype(BF16), rs_ref[j]) for j in heads]
    for j in heads:
        c = columns(j)
        whole = dfk[j] + dfk_ref[:, c] + head_row(rz_ref, step, j)
        gk_ref[:, c] = (whole * jnp.minimum(fk32[j], 1.0)).astype(BF16)
    for j in heads:
        c = columns(j)
        gv_out_ref[:, c] = (gv[j] + gv_ref[:, c]).astype(BF16)


def head_call(kernel, step, kinds_in, kinds_out, arrays, tokens, heads):
    wide = pl.BlockSpec((tokens, step * HD), lambda i: (0, i))
    square = pl.BlockSpec((step, HD, HD), lambda i: (i, 0, 0))
    rows = pl.BlockSpec((heads, HD), lambda i: (0, 0))
    specs = {"w": wide, "f": wide, "s": square, "r": rows}
    shapes = {
        "w": jax.ShapeDtypeStruct((tokens, heads * HD), BF16),
        "f": jax.ShapeDtypeStruct((tokens, heads * HD), F32),
        "s": jax.ShapeDtypeStruct((heads, HD, HD), BF16),
        "r": jax.ShapeDtypeStruct((heads, HD), F32),
    }
    return pl.pallas_call(
        functools.partial(kernel, step),
        grid=(heads // step,),
        in_specs=[specs[t] for t in kinds_in],
        out_specs=[specs[t] for t in kinds_out],
        out_shape=[shapes[t] for t in kinds_out],
        compiler_params=pltpu.CompilerParams(dimension_semantics=("arbitrary",)),
    )(*arrays)


def z_total_kernel(x_ref, tot_ref):
    tot = x_ref[0].astype(F32)
    for z in range(1, x_ref.shape[0]):
        tot = tot + x_ref[z].astype(F32)
    tot_ref[...] = tot


def z_running_kernel(forward, x_ref, base_ref, out_ref):
    n = x_ref.shape[0]
    acc = base_ref[...]
    for s in range(n):
        z = s if forward else n - 1 - s
        out_ref[z] = acc.astype(BF16)
        if s < n - 1:
            acc = acc + x_ref[z].astype(F32)


def z_total(x):
    n, rows, lanes = x.shape
    return pl.pallas_call(
        z_total_kernel,
        grid=(1,),
        in_specs=[pl.BlockSpec((n, rows, lanes), lambda i: (0, i, 0))],
        out_specs=pl.BlockSpec((rows, lanes), lambda i: (i, 0)),
        out_shape=jax.ShapeDtypeStruct((rows, lanes), F32),
    )(x)


def z_running(x, base, forward):
    n, rows, lanes = x.shape
    return pl.pallas_call(
        functools.partial(z_running_kernel, forward),
        grid=(1,),
        in_specs=[
            pl.BlockSpec((n, rows, lanes), lambda i: (0, i, 0)),
            pl.BlockSpec((rows, lanes), lambda i: (i, 0)),
        ],
        out_specs=pl.BlockSpec((n, rows, lanes), lambda i: (0, i, 0)),
        out_shape=jax.ShapeDtypeStruct((n, rows, lanes), BF16),
    )(x, base)


def level(part, total, n, place, hop, forward, wire):
    before = None
    d = 1
    while d < n:
        if total is None:
            got_part, got_total = hop(part.astype(wire), d).astype(F32), None
        elif total is part:
            got_part = got_total = hop(part.astype(wire), d).astype(F32)
        else:
            got = hop(jnp.stack([part, total]).astype(wire), d).astype(F32)
            got_part, got_total = got[0], got[1]
        ok = (place >= d) if forward else (place < n - d)
        masked = jnp.where(ok, got_part, 0.0)
        before = masked if before is None else before + masked
        part, total = part + masked, None if total is None else total + got_total
        d *= 2
    return before, total


def grid_of(ctx):
    side = 1
    while side * side * 2 < ctx:
        side += 1
    return side


def ctx_hop(side, which, forward):
    def hop(value, d):
        d = d if forward else -d
        pairs = []
        for x in range(side):
            for y in range(side):
                for c in range(2):
                    to = (x, (y + d) % side) if which == "y" else ((x + d) % side, y)
                    pairs.append(((x * side + y) * 2 + c, (to[0] * side + to[1]) * 2 + c))
        return lax.ppermute(value, "ctx", pairs)

    return hop


def swap_cores(value, ctx):
    return lax.ppermute(value, "ctx", [(i, i ^ 1) for i in range(ctx)])


def ctx_running(total, ctx, forward, wire, split):
    side = grid_of(ctx)
    place = lax.axis_index("ctx")
    core, y, x = place % 2, (place // 2) % side, place // (2 * side)
    other = swap_cores(total, ctx)
    by_core = jnp.where((core == 1) if forward else (core == 0), other, 0.0)
    chip = total + other
    half = total.shape[0] // 2
    if split:
        chip = jnp.where(core == 0, chip[:half], chip[half:])
    by_y, row = level(chip, chip, side, y, ctx_hop(side, "y", forward), forward, wire)
    by_x, _ = level(row, None, side, x, ctx_hop(side, "x", forward), forward, wire)
    base = by_y + by_x
    if split:
        got = swap_cores(base, ctx)
        base = jnp.concatenate([jnp.where(core == 0, base, got), jnp.where(core == 0, got, base)])
    return by_core + base


def z_gather(x, group):
    return lax.all_to_all(jnp.broadcast_to(x[None], (group, *x.shape)), "head", 0, 0, tiled=True)


def shards(ctx, group, queries, keys, values, out_grad):
    tokens, width = queries.shape
    heads = width // HD
    call = functools.partial(head_call, tokens=tokens, heads=heads)
    owned = heads * HD // group
    place = lax.axis_index("head")

    def to_owners(state):
        return lax.all_to_all(state.reshape(group, owned, HD), "head", 0, 0, tiled=True)

    def from_owners(x):
        return lax.all_to_all(x, "head", 0, 0, tiled=True).reshape(heads, HD, HD)

    ranks = jnp.arange(group)[:, None, None]
    key_state, key_sum = call(key_state_kernel, 16, "ww", "sr", (keys, values))
    key_parts = to_owners(key_state)
    earlier = ctx_running(key_sum, ctx, True, F32, False)
    key_parts, both = lax.optimization_barrier((key_parts, jnp.stack([key_sum, earlier])))
    sums = z_gather(both, group)
    z = jnp.sum(sums[:, 1], axis=0) + jnp.sum(jnp.where(ranks < place, sums[:, 0], 0.0), axis=0)
    (query_state,) = call(query_state_kernel, 16, "wwwr", "s", (queries, keys, out_grad, z))
    query_parts = to_owners(query_state)
    key_total = z_total(key_parts)
    key_base = ctx_running(key_total, ctx, True, BF16, True)
    key_running = z_running(key_parts, key_base, True)
    query_parts, key_running = lax.optimization_barrier((query_parts, key_running))
    prefix = from_owners(key_running)
    query_total = z_total(query_parts)
    query_base = ctx_running(query_total, ctx, False, BF16, True)
    query_running = z_running(query_parts, query_base, False)
    locals_in = (queries, keys, values, out_grad, z, prefix)
    (query_sum,) = call(query_sum_kernel, 16, "wwwwrs", "r", locals_in)
    sums = z_gather(query_sum, group)
    sums, query_running = lax.optimization_barrier((sums, query_running))
    grad_queries, dfk, gv = call(query_grad_kernel, 8, "wwwwrs", "wff", locals_in)
    suffix = from_owners(query_running)
    r = ctx_running(jnp.sum(sums, axis=0), ctx, False, F32, False)
    r = r + jnp.sum(jnp.where(ranks > place, sums, 0.0), axis=0)
    grad_keys, grad_values = call(
        key_grad_kernel, 16, "wwffsr", "ww", (keys, values, dfk, gv, suffix, r)
    )
    return grad_queries, grad_keys, grad_values


def solution(mesh):
    spec = P(("ctx", "head"), None)
    body = functools.partial(shards, mesh.shape["ctx"], mesh.shape["head"])

    return jax.shard_map(
        body, mesh=mesh, in_specs=(spec,) * 4, out_specs=(spec,) * 3, check_vma=False
    )
```

```python
import functools

import jax
import jax.numpy as jnp
from jax import lax
from jax.experimental import pallas as pl
from jax.experimental.pallas import tpu as pltpu
from jax.sharding import PartitionSpec as P

HD = 128

F32 = jnp.float32
BF16 = jnp.bfloat16


def feature(real):
    return jnp.where(real > 0, real + 1.0, jnp.exp(jnp.minimum(real, 0.0)))


def dot_nn(a, b):
    return lax.dot_general(a, b, (((1,), (0,)), ((), ())), preferred_element_type=F32)


def dot_nt(a, b):
    return lax.dot_general(a, b, (((1,), (1,)), ((), ())), preferred_element_type=F32)


def dot_tn(a, b):
    return lax.dot_general(a, b, (((0,), (0,)), ((), ())), preferred_element_type=F32)


def causal(n):
    return lax.broadcasted_iota(jnp.int32, (n, n), 0) >= lax.broadcasted_iota(jnp.int32, (n, n), 1)


def columns(j):
    return slice(j * HD, (j + 1) * HD)


def head_row(ref, step, j):
    return ref[pl.ds(pl.program_id(0) * step + j, 1), :]


def put_rows(ref, step, j, row):
    at = pl.ds(pl.program_id(0) * step + j, 1)
    for member in range(ref.shape[0]):
        ref[member, at, :] = row


def each(fn, *lists):
    return [fn(*items) for items in zip(*lists)]


def key_state_kernel(step, k_ref, v_ref, state_ref, sum_ref):
    heads = range(step)
    fk = [feature(k_ref[:, columns(j)].astype(F32)).astype(BF16) for j in heads]
    states = [dot_tn(fk[j], v_ref[:, columns(j)]) for j in heads]
    for j in heads:
        row = jnp.sum(fk[j].astype(F32), axis=0, keepdims=True)
        put_rows(sum_ref, step, j, row)
    for j in heads:
        state_ref[j] = states[j].astype(BF16)


def scores_of(fq, fk, zrows, mask):
    scores = [jnp.where(mask, s, 0.0) for s in each(dot_nt, fq, fk)]
    dens = [
        jnp.sum(s + f.astype(F32) * zrow, axis=1, keepdims=True)
        for s, f, zrow in zip(scores, fq, zrows)
    ]
    return [s.astype(BF16) for s in scores], [1.0 / den for den in dens]


def query_state_kernel(step, q_ref, k_ref, g_ref, z_ref, state_ref):
    mask = causal(q_ref.shape[0])
    heads = range(step)
    fq = [feature(q_ref[:, columns(j)].astype(F32)).astype(BF16) for j in heads]
    fk = [feature(k_ref[:, columns(j)].astype(F32)).astype(BF16) for j in heads]
    _, inverse = scores_of(fq, fk, [head_row(z_ref, step, j) for j in heads], mask)
    dnum = [(g_ref[:, columns(j)].astype(F32) * inverse[j]).astype(BF16) for j in heads]
    states = each(dot_tn, fq, dnum)
    for j in heads:
        state_ref[j] = states[j].astype(BF16)


def num_of(fq, weights, v, s_ref):
    return [dot_nn(w, x) + dot_nn(f, s_ref[j]) for j, (f, w, x) in enumerate(zip(fq, weights, v))]


def dden_of(g_ref, num, inverse):
    shared = [
        jnp.sum(g_ref[:, columns(j)].astype(F32) * n, axis=1, keepdims=True)
        for j, n in enumerate(num)
    ]
    return [-(s * i) * i for s, i in zip(shared, inverse)]


def query_grad_kernel(step, q_ref, k_ref, v_ref, g_ref, z_ref, s_ref, gq_ref, dfk_ref, gv_ref, sum_ref):
    mask = causal(q_ref.shape[0])
    heads = range(step)
    fq32 = [feature(q_ref[:, columns(j)].astype(F32)) for j in heads]
    fq = [f.astype(BF16) for f in fq32]
    fk = [feature(k_ref[:, columns(j)].astype(F32)).astype(BF16) for j in heads]
    zrows = [head_row(z_ref, step, j) for j in heads]
    v = [v_ref[:, columns(j)] for j in heads]
    weights, inverse = scores_of(fq, fk, zrows, mask)
    num = num_of(fq, weights, v, s_ref)
    dnum = [(g_ref[:, columns(j)].astype(F32) * inverse[j]).astype(BF16) for j in heads]
    pair = each(dot_nt, dnum, v)
    dden = dden_of(g_ref, num, inverse)
    mixing = [jnp.where(mask, p + d, 0.0).astype(BF16) for p, d in zip(pair, dden)]
    for j in heads:
        row = jnp.sum(dden[j] * fq[j].astype(F32), axis=0, keepdims=True)
        put_rows(sum_ref, step, j, row)
    for j in heads:
        gv_ref[:, columns(j)] = dot_tn(weights[j], dnum[j])
    dfq = [
        dot_nn(mixing[j], fk[j]) + dot_nt(dnum[j], s_ref[j]) + dden[j] * zrows[j] for j in heads
    ]
    for j in heads:
        gq_ref[:, columns(j)] = (dfq[j] * jnp.minimum(fq32[j], 1.0)).astype(BF16)
    for j in heads:
        dfk_ref[:, columns(j)] = dot_tn(mixing[j], fq[j])


def key_grad_kernel(
    place_ref, k_ref, v_ref, dfk_ref, gv_ref, rz_ref, *refs
):
    pieces, (gk_ref, gv_out_ref) = refs[:-2], refs[-2:]
    group = len(pieces)
    per = pieces[0].shape[0] // HD
    for first in range(0, group, 2):
        work = []
        for d in (first, first + 1):
            owner = lax.rem(place_ref[0] + group - d, group)
            for j in range(per):
                at = pl.ds(pl.multiple_of(owner * per * HD, per * HD) + j * HD, HD)
                work.append((pieces[d][j * HD : (j + 1) * HD, :], at, owner * per + j))
        fk32 = [feature(k_ref[:, at].astype(F32)) for _, at, _ in work]
        dfk = [dot_nt(v_ref[:, at], state) for state, at, _ in work]
        gv = [dot_nn(f.astype(BF16), state) for f, (state, _, _) in zip(fk32, work)]
        for f, whole, (_, at, head) in zip(fk32, dfk, work):
            whole = whole + dfk_ref[:, at] + rz_ref[pl.ds(head, 1), :]
            gk_ref[:, at] = (whole * jnp.minimum(f, 1.0)).astype(BF16)
        for part, (_, at, _) in zip(gv, work):
            gv_out_ref[:, at] = (part + gv_ref[:, at]).astype(BF16)


def key_grad(place, arrays, pieces, tokens, width):
    return pl.pallas_call(
        key_grad_kernel,
        in_specs=[pl.BlockSpec(memory_space=pltpu.SMEM)]
        + [pl.BlockSpec(memory_space=pltpu.VMEM)] * (len(arrays) + len(pieces)),
        out_specs=[pl.BlockSpec(memory_space=pltpu.VMEM)] * 2,
        out_shape=[jax.ShapeDtypeStruct((tokens, width), BF16)] * 2,
    )(place, *arrays, *pieces)


def head_call(kernel, step, kinds_in, kinds_out, arrays, tokens, heads, group):
    wide = pl.BlockSpec((tokens, step * HD), lambda i: (0, i))
    square = pl.BlockSpec((step, HD, HD), lambda i: (i, 0, 0))
    rows = pl.BlockSpec((heads, HD), lambda i: (0, 0))
    copies = pl.BlockSpec((group, heads, HD), lambda i: (0, 0, 0))
    specs = {"g": copies, "w": wide, "f": wide, "s": square, "r": rows}
    shapes = {
        "g": jax.ShapeDtypeStruct((group, heads, HD), F32),
        "w": jax.ShapeDtypeStruct((tokens, heads * HD), BF16),
        "f": jax.ShapeDtypeStruct((tokens, heads * HD), F32),
        "s": jax.ShapeDtypeStruct((heads, HD, HD), BF16),
        "r": jax.ShapeDtypeStruct((heads, HD), F32),
    }
    return pl.pallas_call(
        functools.partial(kernel, step),
        grid=(heads // step,),
        in_specs=[specs[t] for t in kinds_in],
        out_specs=[specs[t] for t in kinds_out],
        out_shape=[shapes[t] for t in kinds_out],
        compiler_params=pltpu.CompilerParams(dimension_semantics=("arbitrary",)),
    )(*arrays)


def z_total_kernel(x_ref, tot_ref):
    tot = x_ref[0].astype(F32)
    for z in range(1, x_ref.shape[0]):
        tot = tot + x_ref[z].astype(F32)
    tot_ref[...] = tot


def z_running_kernel(forward, x_ref, base_ref, out_ref):
    n = x_ref.shape[0]
    acc = base_ref[...]
    for s in range(n):
        z = s if forward else n - 1 - s
        out_ref[z] = acc.astype(BF16)
        if s < n - 1:
            acc = acc + x_ref[z].astype(F32)


def z_total(x):
    n, rows, lanes = x.shape
    return pl.pallas_call(
        z_total_kernel,
        grid=(1,),
        in_specs=[pl.BlockSpec((n, rows, lanes), lambda i: (0, i, 0))],
        out_specs=pl.BlockSpec((rows, lanes), lambda i: (i, 0)),
        out_shape=jax.ShapeDtypeStruct((rows, lanes), F32),
    )(x)


def z_spread_kernel(place_ref, x_ref, base_ref, *refs):
    outs, held = refs[:-1], refs[-1]
    z_running_kernel(False, x_ref, base_ref, held)
    for d, out in enumerate(outs):
        out[...] = held[lax.rem(place_ref[0] + d, len(outs))]


def z_running(x, base, forward):
    n, rows, lanes = x.shape
    whole = pl.BlockSpec(memory_space=pltpu.VMEM)
    return pl.pallas_call(
        functools.partial(z_running_kernel, forward),
        in_specs=[whole, whole],
        out_specs=whole,
        out_shape=jax.ShapeDtypeStruct((n, rows, lanes), BF16),
    )(x, base)


def z_spread(place, x, base):
    n, rows, lanes = x.shape
    whole = pl.BlockSpec(memory_space=pltpu.VMEM)
    return pl.pallas_call(
        z_spread_kernel,
        in_specs=[pl.BlockSpec(memory_space=pltpu.SMEM), whole, whole],
        out_specs=[whole] * n,
        out_shape=[jax.ShapeDtypeStruct((rows, lanes), BF16)] * n,
        scratch_shapes=[pltpu.VMEM((n, rows, lanes), BF16)],
    )(place, x, base)


def level(value, n, place, hop, forward, wire, need_total):
    sent = value.astype(wire)
    got = [hop(sent, d, need_total).astype(F32) for d in range(1, n)]
    if not need_total:
        return sum(got[1:], got[0]), None
    before = sum(
        jnp.where((place >= d) if forward else (place < n - d), g, 0.0) for d, g in enumerate(got, 1)
    )
    return before, sum(got, value)


def grid_of(ctx):
    side = 1
    while side * side * 2 < ctx:
        side += 1
    return side


def ctx_hop(side, which, forward):
    def hop(value, d, wrap):
        d = d if forward else -d
        pairs = []
        for x in range(side):
            for y in range(side):
                to = (x, y + d) if which == "y" else (x + d, y)
                if not wrap and not all(0 <= t < side for t in to):
                    continue
                at = (to[0] % side) * side + to[1] % side
                pairs += [((x * side + y) * 2 + c, at * 2 + c) for c in range(2)]
        return lax.ppermute(value, "ctx", pairs)

    return hop


def swap_cores(value, ctx):
    return lax.ppermute(value, "ctx", [(i, i ^ 1) for i in range(ctx)])


def ctx_running(total, ctx, forward, wire, split):
    side = grid_of(ctx)
    place = lax.axis_index("ctx")
    core, y, x = place % 2, (place // 2) % side, place // (2 * side)
    other = swap_cores(total, ctx)
    by_core = jnp.where((core == 1) if forward else (core == 0), other, 0.0)
    chip = total + other
    half = total.shape[0] // 2
    if split:
        chip = jnp.where(core == 0, chip[:half], chip[half:])
    by_y, row = level(chip, side, y, ctx_hop(side, "y", forward), forward, wire, True)
    by_x, _ = level(row, side, x, ctx_hop(side, "x", forward), forward, wire, False)
    base = by_y + by_x
    if split:
        got = swap_cores(base, ctx)
        base = jnp.concatenate([jnp.where(core == 0, base, got), jnp.where(core == 0, got, base)])
    return by_core + base


def z_gather(copies):
    return lax.all_to_all(copies, "head", 0, 0, tiled=True)


def shards(ctx, group, queries, keys, values, out_grad):
    tokens, width = queries.shape
    heads = width // HD
    call = functools.partial(head_call, tokens=tokens, heads=heads, group=group)
    owned = heads * HD // group
    place = lax.axis_index("head")

    def to_owners(state):
        return lax.all_to_all(state.reshape(group, owned, HD), "head", 0, 0, tiled=True)

    def from_owners(x):
        return lax.all_to_all(x, "head", 0, 0, tiled=True).reshape(heads, HD, HD)

    ranks = jnp.arange(group)[:, None, None]
    where = jnp.full((1,), place, jnp.int32)
    key_state, key_sum = call(key_state_kernel, 16, "ww", "sg", (keys, values))
    sums = z_gather(key_sum)
    before = jnp.sum(jnp.where(ranks < place, sums, 0.0), axis=0)
    total = jnp.sum(sums, axis=0)
    key_state, before, total = lax.optimization_barrier((key_state, before, total))
    key_parts = to_owners(key_state)
    z = before + ctx_running(total, ctx, True, F32, False)
    (query_state,) = call(query_state_kernel, 16, "wwwr", "s", (queries, keys, out_grad, z))
    key_parts, query_state = lax.optimization_barrier((key_parts, query_state))
    query_parts = to_owners(query_state)
    key_total = z_total(key_parts)
    key_base = ctx_running(key_total, ctx, True, BF16, True)
    key_running = z_running(key_parts, key_base, True)
    query_parts, key_running = lax.optimization_barrier((query_parts, key_running))
    prefix = from_owners(key_running)
    query_total = z_total(query_parts)
    query_base = ctx_running(query_total, ctx, False, BF16, True)
    spread = z_spread(where, query_parts, query_base)
    grad_queries, dfk, gv, query_sum = call(
        query_grad_kernel, 8, "wwwwrs", "wffg", (queries, keys, values, out_grad, z, prefix)
    )
    sums = z_gather(query_sum)
    pieces = [spread[0]] + [None] * (group - 1)
    for d in sorted(range(1, group), key=lambda d: -min(d, group - d)):
        pairs = [(i, (i + d) % group) for i in range(group)]
        pieces[d] = lax.ppermute(spread[d], "head", pairs)
    r = ctx_running(jnp.sum(sums, axis=0), ctx, False, F32, False)
    r = r + jnp.sum(jnp.where(ranks > place, sums, 0.0), axis=0)
    grad_keys, grad_values = key_grad(
        where, (keys, values, dfk, gv, r), pieces, tokens, width
    )
    return grad_queries, grad_keys, grad_values


def solution(mesh):
    spec = P(("ctx", "head"), None)
    body = functools.partial(shards, mesh.shape["ctx"], mesh.shape["head"])

    return jax.shard_map(
        body, mesh=mesh, in_specs=(spec,) * 4, out_specs=(spec,) * 3, check_vma=False
    )
```

```python
import functools

import jax
import jax.numpy as jnp
from jax import lax
from jax.experimental import pallas as pl
from jax.experimental.pallas import tpu as pltpu
from jax.sharding import PartitionSpec as P

HD = 128

F32 = jnp.float32
BF16 = jnp.bfloat16


def feature(real):
    return jnp.where(real > 0, real + 1.0, jnp.exp(jnp.minimum(real, 0.0)))


def dot_nn(a, b):
    return lax.dot_general(a, b, (((1,), (0,)), ((), ())), preferred_element_type=F32)


def dot_nt(a, b):
    return lax.dot_general(a, b, (((1,), (1,)), ((), ())), preferred_element_type=F32)


def dot_tn(a, b):
    return lax.dot_general(a, b, (((0,), (0,)), ((), ())), preferred_element_type=F32)


def causal(n):
    return lax.broadcasted_iota(jnp.int32, (n, n), 0) >= lax.broadcasted_iota(jnp.int32, (n, n), 1)


def columns(j):
    return slice(j * HD, (j + 1) * HD)


def head_row(ref, step, j):
    return ref[pl.ds(pl.program_id(0) * step + j, 1), :]


def put_rows(ref, step, j, row):
    at = pl.ds(pl.program_id(0) * step + j, 1)
    for member in range(ref.shape[0]):
        ref[member, at, :] = row


def each(fn, *lists):
    return [fn(*items) for items in zip(*lists)]


def key_state_kernel(step, k_ref, v_ref, state_ref, sum_ref):
    heads = range(step)
    fk = [feature(k_ref[:, columns(j)].astype(F32)).astype(BF16) for j in heads]
    states = [dot_tn(fk[j], v_ref[:, columns(j)]) for j in heads]
    for j in heads:
        row = jnp.sum(fk[j].astype(F32), axis=0, keepdims=True)
        put_rows(sum_ref, step, j, row)
    for j in heads:
        state_ref[j] = states[j].astype(BF16)


def scores_of(fq, fk, zrows, mask):
    scores = [jnp.where(mask, s, 0.0) for s in each(dot_nt, fq, fk)]
    dens = [
        jnp.sum(s + f.astype(F32) * zrow, axis=1, keepdims=True)
        for s, f, zrow in zip(scores, fq, zrows)
    ]
    return [s.astype(BF16) for s in scores], [1.0 / den for den in dens]


def query_state_kernel(step, q_ref, k_ref, g_ref, z_ref, state_ref):
    mask = causal(q_ref.shape[0])
    heads = range(step)
    fq = [feature(q_ref[:, columns(j)].astype(F32)).astype(BF16) for j in heads]
    fk = [feature(k_ref[:, columns(j)].astype(F32)).astype(BF16) for j in heads]
    _, inverse = scores_of(fq, fk, [head_row(z_ref, step, j) for j in heads], mask)
    dnum = [(g_ref[:, columns(j)].astype(F32) * inverse[j]).astype(BF16) for j in heads]
    states = each(dot_tn, fq, dnum)
    for j in heads:
        state_ref[j] = states[j].astype(BF16)


def num_of(fq, weights, v, s_ref):
    return [dot_nn(w, x) + dot_nn(f, s_ref[j]) for j, (f, w, x) in enumerate(zip(fq, weights, v))]


def dden_of(g_ref, num, inverse):
    shared = [
        jnp.sum(g_ref[:, columns(j)].astype(F32) * n, axis=1, keepdims=True)
        for j, n in enumerate(num)
    ]
    return [-(s * i) * i for s, i in zip(shared, inverse)]


def query_grad_kernel(step, q_ref, k_ref, v_ref, g_ref, z_ref, s_ref, gq_ref, dfk_ref, gv_ref, sum_ref):
    mask = causal(q_ref.shape[0])
    heads = range(step)
    fq32 = [feature(q_ref[:, columns(j)].astype(F32)) for j in heads]
    fq = [f.astype(BF16) for f in fq32]
    fk = [feature(k_ref[:, columns(j)].astype(F32)).astype(BF16) for j in heads]
    zrows = [head_row(z_ref, step, j) for j in heads]
    v = [v_ref[:, columns(j)] for j in heads]
    weights, inverse = scores_of(fq, fk, zrows, mask)
    num = num_of(fq, weights, v, s_ref)
    dnum = [(g_ref[:, columns(j)].astype(F32) * inverse[j]).astype(BF16) for j in heads]
    pair = each(dot_nt, dnum, v)
    dden = dden_of(g_ref, num, inverse)
    mixing = [jnp.where(mask, p + d, 0.0).astype(BF16) for p, d in zip(pair, dden)]
    for j in heads:
        row = jnp.sum(dden[j] * fq[j].astype(F32), axis=0, keepdims=True)
        put_rows(sum_ref, step, j, row)
    for j in heads:
        gv_ref[:, columns(j)] = dot_tn(weights[j], dnum[j])
    dfq = [
        dot_nn(mixing[j], fk[j]) + dot_nt(dnum[j], s_ref[j]) + dden[j] * zrows[j] for j in heads
    ]
    for j in heads:
        gq_ref[:, columns(j)] = (dfq[j] * jnp.minimum(fq32[j], 1.0)).astype(BF16)
    for j in heads:
        dfk_ref[:, columns(j)] = dot_tn(mixing[j], fq[j])


def key_grad_kernel(place_ref, k_hbm, v_hbm, dfk_hbm, gv_hbm, rz_ref, *refs):
    group = len(refs) - 7
    pieces, (gk_ref, gv_out_ref), loaded, sems = refs[:group], refs[group : group + 2], refs[-5:-1], refs[-1]
    rows = pieces[0].shape[0]
    owners = [lax.rem(place_ref[0] + group - d, group) for d in range(group)]
    ats = [pl.multiple_of(owner * rows, rows) for owner in owners]
    copies = [
        [
            pltpu.make_async_copy(src.at[:, pl.ds(at, rows)], dst.at[d], sems.at[n, d])
            for n, (src, dst) in enumerate(zip((k_hbm, v_hbm, dfk_hbm, gv_hbm), loaded))
        ]
        for d, at in enumerate(ats)
    ]
    for some in copies:
        for copy in some:
            copy.start()
    k, v, dfk_in, gv_in = loaded
    for first in range(0, group, 2):
        work = []
        for d in (first, first + 1):
            for copy in copies[d]:
                copy.wait()
            work += [(d, j) for j in range(rows // HD)]
        states = [pieces[d][columns(j), :] for d, j in work]
        fk32 = [feature(k[d, :, columns(j)].astype(F32)) for d, j in work]
        dfk = [dot_nt(v[d, :, columns(j)], state) for (d, j), state in zip(work, states)]
        gv = [dot_nn(f.astype(BF16), state) for f, state in zip(fk32, states)]
        for f, whole, (d, j) in zip(fk32, dfk, work):
            row = rz_ref[pl.ds(owners[d] * (rows // HD) + j, 1), :]
            whole = whole + dfk_in[d, :, columns(j)] + row
            gk_ref[:, pl.ds(ats[d] + j * HD, HD)] = (whole * jnp.minimum(f, 1.0)).astype(BF16)
        for part, (d, j) in zip(gv, work):
            part = part + gv_in[d, :, columns(j)]
            gv_out_ref[:, pl.ds(ats[d] + j * HD, HD)] = part.astype(BF16)


def key_grad(place, k, v, dfk, gv, r, pieces):
    tokens, width = k.shape
    group, rows = len(pieces), pieces[0].shape[0]
    whole, away = pl.BlockSpec(memory_space=pltpu.VMEM), pl.BlockSpec(memory_space=pl.ANY)
    return pl.pallas_call(
        key_grad_kernel,
        in_specs=[pl.BlockSpec(memory_space=pltpu.SMEM)] + [away] * 4 + [whole] * (1 + group),
        out_specs=[whole] * 2,
        out_shape=[jax.ShapeDtypeStruct((tokens, width), BF16)] * 2,
        scratch_shapes=[pltpu.VMEM((group, tokens, rows), x.dtype) for x in (k, v, dfk, gv)]
        + [pltpu.SemaphoreType.DMA((4, group))],
    )(place, k, v, dfk, gv, r, *pieces)


def head_call(kernel, step, kinds_in, kinds_out, arrays, tokens, heads, group):
    wide = pl.BlockSpec((tokens, step * HD), lambda i: (0, i))
    square = pl.BlockSpec((step, HD, HD), lambda i: (i, 0, 0))
    rows = pl.BlockSpec((heads, HD), lambda i: (0, 0))
    copies = pl.BlockSpec((group, heads, HD), lambda i: (0, 0, 0))
    specs = {"g": copies, "w": wide, "f": wide, "s": square, "r": rows}
    shapes = {
        "g": jax.ShapeDtypeStruct((group, heads, HD), F32),
        "w": jax.ShapeDtypeStruct((tokens, heads * HD), BF16),
        "f": jax.ShapeDtypeStruct((tokens, heads * HD), F32),
        "s": jax.ShapeDtypeStruct((heads, HD, HD), BF16),
        "r": jax.ShapeDtypeStruct((heads, HD), F32),
    }
    return pl.pallas_call(
        functools.partial(kernel, step),
        grid=(heads // step,),
        in_specs=[specs[t] for t in kinds_in],
        out_specs=[specs[t] for t in kinds_out],
        out_shape=[shapes[t] for t in kinds_out],
        compiler_params=pltpu.CompilerParams(dimension_semantics=("arbitrary",)),
    )(*arrays)


def z_running_kernel(forward, x_ref, base_ref, out_ref):
    n = x_ref.shape[0]
    acc = base_ref[...]
    for s in range(n):
        z = s if forward else n - 1 - s
        out_ref[z] = acc.astype(BF16)
        if s < n - 1:
            acc = acc + x_ref[z].astype(F32)


def z_total(x):
    return jnp.sum(x.astype(F32), axis=0)


def z_spread_kernel(place_ref, x_ref, base_ref, *refs):
    outs, held = refs[:-1], refs[-1]
    z_running_kernel(False, x_ref, base_ref, held)
    for d, out in enumerate(outs):
        out[...] = held[lax.rem(place_ref[0] + d, len(outs))]


def z_running(x, base, forward):
    n, rows, lanes = x.shape
    whole = pl.BlockSpec(memory_space=pltpu.VMEM)
    return pl.pallas_call(
        functools.partial(z_running_kernel, forward),
        in_specs=[whole, whole],
        out_specs=whole,
        out_shape=jax.ShapeDtypeStruct((n, rows, lanes), BF16),
    )(x, base)


def z_spread(place, x, base):
    n, rows, lanes = x.shape
    whole = pl.BlockSpec(memory_space=pltpu.VMEM)
    return pl.pallas_call(
        z_spread_kernel,
        in_specs=[pl.BlockSpec(memory_space=pltpu.SMEM), whole, whole],
        out_specs=[whole] * n,
        out_shape=[jax.ShapeDtypeStruct((rows, lanes), BF16)] * n,
        scratch_shapes=[pltpu.VMEM((n, rows, lanes), BF16)],
    )(place, x, base)


def level(value, n, place, hop, forward, wire, need_total):
    sent = value.astype(wire)
    got = [hop(sent, d, need_total).astype(F32) for d in range(1, n)]
    if not need_total:
        return sum(got[1:], got[0]), None
    before = sum(
        jnp.where((place >= d) if forward else (place < n - d), g, 0.0) for d, g in enumerate(got, 1)
    )
    return before, sum(got, value)


def grid_of(ctx):
    side = 1
    while side * side * 2 < ctx:
        side += 1
    return side


def ctx_hop(side, which, forward):
    def hop(value, d, wrap):
        d = d if forward else -d
        pairs = []
        for x in range(side):
            for y in range(side):
                to = (x, y + d) if which == "y" else (x + d, y)
                if not wrap and not all(0 <= t < side for t in to):
                    continue
                at = (to[0] % side) * side + to[1] % side
                pairs += [((x * side + y) * 2 + c, at * 2 + c) for c in range(2)]
        return lax.ppermute(value, "ctx", pairs)

    return hop


def swap_cores(value, ctx):
    return lax.ppermute(value, "ctx", [(i, i ^ 1) for i in range(ctx)])


def ctx_running(total, ctx, forward, wire, split):
    side = grid_of(ctx)
    place = lax.axis_index("ctx")
    core, y, x = place % 2, (place // 2) % side, place // (2 * side)
    other = swap_cores(total, ctx)
    by_core = jnp.where((core == 1) if forward else (core == 0), other, 0.0)
    chip = total + other
    half = total.shape[0] // 2
    if split:
        chip = jnp.where(core == 0, chip[:half], chip[half:])
    by_y, row = level(chip, side, y, ctx_hop(side, "y", forward), forward, wire, True)
    by_x, _ = level(row, side, x, ctx_hop(side, "x", forward), forward, wire, False)
    base = by_y + by_x
    if split:
        got = swap_cores(base, ctx)
        base = jnp.concatenate([jnp.where(core == 0, base, got), jnp.where(core == 0, got, base)])
    return by_core + base


def z_gather(copies):
    return lax.all_to_all(copies, "head", 0, 0, tiled=True)


def shards(ctx, group, queries, keys, values, out_grad):
    tokens, width = queries.shape
    heads = width // HD
    call = functools.partial(head_call, tokens=tokens, heads=heads, group=group)
    owned = heads * HD // group
    place = lax.axis_index("head")

    def to_owners(state):
        return lax.all_to_all(state.reshape(group, owned, HD), "head", 0, 0, tiled=True)

    def from_owners(x):
        return lax.all_to_all(x, "head", 0, 0, tiled=True).reshape(heads, HD, HD)

    ranks = jnp.arange(group)[:, None, None]
    where = jnp.full((1,), place, jnp.int32)
    key_state, key_sum = call(key_state_kernel, 16, "ww", "sg", (keys, values))
    sums = z_gather(key_sum)
    before = jnp.sum(jnp.where(ranks < place, sums, 0.0), axis=0)
    total = jnp.sum(sums, axis=0)
    key_state, before, total = lax.optimization_barrier((key_state, before, total))
    key_parts = to_owners(key_state)
    z = before + ctx_running(total, ctx, True, F32, False)
    (query_state,) = call(query_state_kernel, 16, "wwwr", "s", (queries, keys, out_grad, z))
    key_parts, query_state = lax.optimization_barrier((key_parts, query_state))
    query_parts = to_owners(query_state)
    key_total = z_total(key_parts)
    key_base = ctx_running(key_total, ctx, True, BF16, True)
    key_running = z_running(key_parts, key_base, True)
    query_parts, key_running = lax.optimization_barrier((query_parts, key_running))
    prefix = from_owners(key_running)
    query_total = z_total(query_parts)
    query_base = ctx_running(query_total, ctx, False, BF16, True)
    spread = z_spread(where, query_parts, query_base)
    grad_queries, dfk, gv, query_sum = call(
        query_grad_kernel, 8, "wwwwrs", "wffg", (queries, keys, values, out_grad, z, prefix)
    )
    sums = z_gather(query_sum)
    pieces = [spread[0]] + [None] * (group - 1)
    for d in sorted(range(1, group), key=lambda d: -min(d, group - d)):
        pairs = [(i, (i + d) % group) for i in range(group)]
        pieces[d] = lax.ppermute(spread[d], "head", pairs)
    r = ctx_running(jnp.sum(sums, axis=0), ctx, False, F32, False)
    r = r + jnp.sum(jnp.where(ranks > place, sums, 0.0), axis=0)
    grad_keys, grad_values = key_grad(where, keys, values, dfk, gv, r, pieces)
    return grad_queries, grad_keys, grad_values


def solution(mesh):
    spec = P(("ctx", "head"), None)
    body = functools.partial(shards, mesh.shape["ctx"], mesh.shape["head"])

    return jax.shard_map(
        body, mesh=mesh, in_specs=(spec,) * 4, out_specs=(spec,) * 3, check_vma=False
    )
```

```python
import functools

import jax
import jax.numpy as jnp
from jax import lax
from jax.experimental import pallas as pl
from jax.experimental.pallas import tpu as pltpu
from jax.sharding import PartitionSpec as P

HD = 128

F32 = jnp.float32
BF16 = jnp.bfloat16

LIMIT = pltpu.CompilerParams(vmem_limit_bytes=50 * 2**20)
LIMIT_LAST = pltpu.CompilerParams(vmem_limit_bytes=50 * 2**20)


def feature(real):
    return jnp.where(real > 0, real + 1.0, jnp.exp(jnp.minimum(real, 0.0)))


def dot_nn(a, b):
    return lax.dot_general(a, b, (((1,), (0,)), ((), ())), preferred_element_type=F32)


def dot_nt(a, b):
    return lax.dot_general(a, b, (((1,), (1,)), ((), ())), preferred_element_type=F32)


def dot_tn(a, b):
    return lax.dot_general(a, b, (((0,), (0,)), ((), ())), preferred_element_type=F32)


def causal(n):
    return lax.broadcasted_iota(jnp.int32, (n, n), 0) >= lax.broadcasted_iota(jnp.int32, (n, n), 1)


def columns(j):
    return slice(j * HD, (j + 1) * HD)


def head_row(ref, step, j):
    return ref[pl.ds(pl.program_id(0) * step + j, 1), :]


def put_rows(ref, step, j, row):
    at = pl.ds(pl.program_id(0) * step + j, 1)
    for member in range(ref.shape[0]):
        ref[member, at, :] = row


def each(fn, *lists):
    return [fn(*items) for items in zip(*lists)]


def key_sum_kernel(step, k_ref, sum_ref):
    for j in range(step):
        fk = feature(k_ref[:, columns(j)].astype(F32)).astype(BF16)
        put_rows(sum_ref, step, j, jnp.sum(fk.astype(F32), axis=0, keepdims=True))


def key_state_kernel(step, k_ref, v_ref, state_ref):
    heads = range(step)
    fk = [feature(k_ref[:, columns(j)].astype(F32)).astype(BF16) for j in heads]
    states = [dot_tn(fk[j], v_ref[:, columns(j)]) for j in heads]
    for j in heads:
        state_ref[j] = states[j].astype(BF16)


def scores_of(fq, fk, zrows, mask):
    scores = [jnp.where(mask, s, 0.0) for s in each(dot_nt, fq, fk)]
    dens = [
        jnp.sum(s + f.astype(F32) * zrow, axis=1, keepdims=True)
        for s, f, zrow in zip(scores, fq, zrows)
    ]
    return [s.astype(BF16) for s in scores], [1.0 / den for den in dens]


def query_state_kernel(step, q_ref, k_ref, g_ref, z_ref, state_ref):
    mask = causal(q_ref.shape[0])
    heads = range(step)
    fq = [feature(q_ref[:, columns(j)].astype(F32)).astype(BF16) for j in heads]
    fk = [feature(k_ref[:, columns(j)].astype(F32)).astype(BF16) for j in heads]
    _, inverse = scores_of(fq, fk, [head_row(z_ref, step, j) for j in heads], mask)
    dnum = [(g_ref[:, columns(j)].astype(F32) * inverse[j]).astype(BF16) for j in heads]
    states = each(dot_tn, fq, dnum)
    for j in heads:
        state_ref[j] = states[j].astype(BF16)


def num_of(fq, weights, v, s_ref):
    return [dot_nn(w, x) + dot_nn(f, s_ref[j]) for j, (f, w, x) in enumerate(zip(fq, weights, v))]


def dden_of(g_ref, num, inverse):
    shared = [
        jnp.sum(g_ref[:, columns(j)].astype(F32) * n, axis=1, keepdims=True)
        for j, n in enumerate(num)
    ]
    return [-(s * i) * i for s, i in zip(shared, inverse)]


def query_grad_kernel(step, q_ref, k_ref, v_ref, g_ref, z_ref, s_away, *refs):
    gq_ref, dfk_ref, gv_ref, sum_ref, s_all, sems = refs
    now = pl.program_id(0)

    def load(i):
        return pltpu.make_async_copy(s_away.at[pl.ds(i * step, step)], s_all.at[i], sems.at[i])

    @pl.when(now == 0)
    def _():
        for i in range(s_all.shape[0]):
            load(i).start()

    mask = causal(q_ref.shape[0])
    heads = range(step)
    fq32 = [feature(q_ref[:, columns(j)].astype(F32)) for j in heads]
    fq = [f.astype(BF16) for f in fq32]
    fk = [feature(k_ref[:, columns(j)].astype(F32)).astype(BF16) for j in heads]
    zrows = [head_row(z_ref, step, j) for j in heads]
    v = [v_ref[:, columns(j)] for j in heads]
    weights, inverse = scores_of(fq, fk, zrows, mask)
    load(now).wait()
    s_ref = s_all.at[now]
    num = num_of(fq, weights, v, s_ref)
    dnum = [(g_ref[:, columns(j)].astype(F32) * inverse[j]).astype(BF16) for j in heads]
    pair = each(dot_nt, dnum, v)
    dden = dden_of(g_ref, num, inverse)
    mixing = [jnp.where(mask, p + d, 0.0).astype(BF16) for p, d in zip(pair, dden)]
    for j in heads:
        row = jnp.sum(dden[j] * fq[j].astype(F32), axis=0, keepdims=True)
        put_rows(sum_ref, step, j, row)
    for j in heads:
        gv_ref[:, columns(j)] = dot_tn(weights[j], dnum[j])
    dfq = [
        dot_nn(mixing[j], fk[j]) + dot_nt(dnum[j], s_ref[j]) + dden[j] * zrows[j] for j in heads
    ]
    for j in heads:
        gq_ref[:, columns(j)] = (dfq[j] * jnp.minimum(fq32[j], 1.0)).astype(BF16)
    for j in heads:
        dfk_ref[:, columns(j)] = dot_tn(mixing[j], fq[j])


def key_grad_kernel(place_ref, k_hbm, v_hbm, dfk_hbm, gv_hbm, rz_ref, *refs):
    group = len(refs) - 8
    pieces, (gk_ref, gv_out_ref), loaded, sems = refs[:group], refs[group : group + 2], refs[-6:-1], refs[-1]
    rows = pieces[0].shape[0]
    owners = [lax.rem(place_ref[0] + group - d, group) for d in range(group)]
    ats = [pl.multiple_of(owner * rows, rows) for owner in owners]
    copies = [
        [
            pltpu.make_async_copy(src.at[:, pl.ds(at, rows)], dst.at[d], sems.at[n, d])
            for n, (src, dst) in enumerate(zip((k_hbm, v_hbm, dfk_hbm, gv_hbm), loaded))
        ]
        + [pltpu.make_async_copy(pieces[d], loaded[-1].at[d], sems.at[4, d])]
        for d, at in enumerate(ats)
    ]
    for some in copies:
        for copy in some:
            copy.start()
    k, v, dfk_in, gv_in, suffix = loaded
    for first in range(0, group, 2):
        work = []
        for d in (first, first + 1):
            for copy in copies[d]:
                copy.wait()
            work += [(d, j) for j in range(rows // HD)]
        states = [suffix[d, columns(j), :] for d, j in work]
        fk32 = [feature(k[d, :, columns(j)].astype(F32)) for d, j in work]
        dfk = [dot_nt(v[d, :, columns(j)], state) for (d, j), state in zip(work, states)]
        gv = [dot_nn(f.astype(BF16), state) for f, state in zip(fk32, states)]
        for f, whole, (d, j) in zip(fk32, dfk, work):
            row = rz_ref[pl.ds(owners[d] * (rows // HD) + j, 1), :]
            whole = whole + dfk_in[d, :, columns(j)] + row
            gk_ref[:, pl.ds(ats[d] + j * HD, HD)] = (whole * jnp.minimum(f, 1.0)).astype(BF16)
        for part, (d, j) in zip(gv, work):
            part = part + gv_in[d, :, columns(j)]
            gv_out_ref[:, pl.ds(ats[d] + j * HD, HD)] = part.astype(BF16)


def key_grad(place, k, v, dfk, gv, r, pieces):
    tokens, width = k.shape
    group, rows = len(pieces), pieces[0].shape[0]
    whole, away = pl.BlockSpec(memory_space=pltpu.VMEM), pl.BlockSpec(memory_space=pl.ANY)
    return pl.pallas_call(
        key_grad_kernel,
        in_specs=[pl.BlockSpec(memory_space=pltpu.SMEM)] + [away] * 4 + [whole] + [away] * group,
        out_specs=[whole] * 2,
        out_shape=[jax.ShapeDtypeStruct((tokens, width), BF16)] * 2,
        scratch_shapes=[pltpu.VMEM((group, tokens, rows), x.dtype) for x in (k, v, dfk, gv)]
        + [pltpu.VMEM((group, rows, HD), BF16), pltpu.SemaphoreType.DMA((5, group))],
        compiler_params=LIMIT_LAST,
    )(place, k, v, dfk, gv, r, *pieces)


def head_call(kernel, step, kinds_in, kinds_out, arrays, tokens, heads, group):
    wide = pl.BlockSpec((tokens, step * HD), lambda i: (0, i))
    square = pl.BlockSpec((step, HD, HD), lambda i: (i, 0, 0))
    rows = pl.BlockSpec((heads, HD), lambda i: (0, 0))
    copies = pl.BlockSpec((group, heads, HD), lambda i: (0, 0, 0))
    specs = {"a": pl.BlockSpec(memory_space=pl.ANY), "g": copies, "w": wide, "f": wide, "s": square, "r": rows}
    shapes = {
        "g": jax.ShapeDtypeStruct((group, heads, HD), F32),
        "w": jax.ShapeDtypeStruct((tokens, heads * HD), BF16),
        "f": jax.ShapeDtypeStruct((tokens, heads * HD), F32),
        "s": jax.ShapeDtypeStruct((heads, HD, HD), BF16),
        "r": jax.ShapeDtypeStruct((heads, HD), F32),
    }
    return pl.pallas_call(
        functools.partial(kernel, step),
        grid=(heads // step,),
        in_specs=[specs[t] for t in kinds_in],
        out_specs=[specs[t] for t in kinds_out],
        out_shape=[shapes[t] for t in kinds_out],
        scratch_shapes=[
            pltpu.VMEM((heads // step, step, HD, HD), BF16),
            pltpu.SemaphoreType.DMA((heads // step,)),
        ]
        if "a" in kinds_in
        else [],
        compiler_params=LIMIT if "a" in kinds_in else None,
    )(*arrays)


def z_running_kernel(forward, x_ref, base_ref, out_ref):
    n = x_ref.shape[0]
    acc = base_ref[...]
    for s in range(n):
        z = s if forward else n - 1 - s
        out_ref[z] = acc.astype(BF16)
        if s < n - 1:
            acc = acc + x_ref[z].astype(F32)


def z_total(x):
    return jnp.sum(x.astype(F32), axis=0)


def z_spread_kernel(place_ref, x_ref, base_ref, *refs):
    outs, held = refs[:-1], refs[-1]
    z_running_kernel(False, x_ref, base_ref, held)
    for d, out in enumerate(outs):
        out[...] = held[lax.rem(place_ref[0] + d, len(outs))]


def z_running(x, base, forward):
    n, rows, lanes = x.shape
    whole = pl.BlockSpec(memory_space=pltpu.VMEM)
    return pl.pallas_call(
        functools.partial(z_running_kernel, forward),
        in_specs=[whole, whole],
        out_specs=whole,
        out_shape=jax.ShapeDtypeStruct((n, rows, lanes), BF16),
    )(x, base)


def z_spread(place, x, base):
    n, rows, lanes = x.shape
    whole = pl.BlockSpec(memory_space=pltpu.VMEM)
    return pl.pallas_call(
        z_spread_kernel,
        in_specs=[pl.BlockSpec(memory_space=pltpu.SMEM), whole, whole],
        out_specs=[whole] * n,
        out_shape=[jax.ShapeDtypeStruct((rows, lanes), BF16)] * n,
        scratch_shapes=[pltpu.VMEM((n, rows, lanes), BF16)],
    )(place, x, base)


def level(value, n, place, hop, forward, wire, need_total):
    sent = value.astype(wire)
    got = [hop(sent, d, need_total).astype(F32) for d in range(1, n)]
    if not need_total:
        return sum(got[1:], got[0]), None
    before = sum(
        jnp.where((place >= d) if forward else (place < n - d), g, 0.0) for d, g in enumerate(got, 1)
    )
    return before, sum(got, value)


def grid_of(ctx):
    side = 1
    while side * side * 2 < ctx:
        side += 1
    return side


def ctx_hop(side, which, forward):
    def hop(value, d, wrap):
        d = d if forward else -d
        pairs = []
        for x in range(side):
            for y in range(side):
                to = (x, y + d) if which == "y" else (x + d, y)
                if not wrap and not all(0 <= t < side for t in to):
                    continue
                at = (to[0] % side) * side + to[1] % side
                pairs += [((x * side + y) * 2 + c, at * 2 + c) for c in range(2)]
        return lax.ppermute(value, "ctx", pairs)

    return hop


def swap_cores(value, ctx):
    return lax.ppermute(value, "ctx", [(i, i ^ 1) for i in range(ctx)])


def ctx_running(total, ctx, forward, wire, split):
    side = grid_of(ctx)
    place = lax.axis_index("ctx")
    core, y, x = place % 2, (place // 2) % side, place // (2 * side)
    other = swap_cores(total, ctx)
    by_core = jnp.where((core == 1) if forward else (core == 0), other, 0.0)
    chip = total + other
    half = total.shape[0] // 2
    if split:
        chip = jnp.where(core == 0, chip[:half], chip[half:])
    by_y, row = level(chip, side, y, ctx_hop(side, "y", forward), forward, wire, True)
    by_x, _ = level(row, side, x, ctx_hop(side, "x", forward), forward, wire, False)
    base = by_y + by_x
    if split:
        got = swap_cores(base, ctx)
        base = jnp.concatenate([jnp.where(core == 0, base, got), jnp.where(core == 0, got, base)])
    return by_core + base


def z_gather(copies):
    return lax.all_to_all(copies, "head", 0, 0, tiled=True)


def shards(ctx, group, queries, keys, values, out_grad):
    tokens, width = queries.shape
    heads = width // HD
    call = functools.partial(head_call, tokens=tokens, heads=heads, group=group)
    owned = heads * HD // group
    place = lax.axis_index("head")

    def to_owners(state):
        return lax.all_to_all(state.reshape(group, owned, HD), "head", 0, 0, tiled=True)

    def from_owners(x):
        return lax.all_to_all(x, "head", 0, 0, tiled=True).reshape(heads, HD, HD)

    ranks = jnp.arange(group)[:, None, None]
    where = jnp.full((1,), place, jnp.int32)
    (key_sum,) = call(key_sum_kernel, 16, "w", "g", (keys,))
    sums = z_gather(key_sum)
    before = jnp.sum(jnp.where(ranks < place, sums, 0.0), axis=0)
    total = jnp.sum(sums, axis=0)
    (key_state,) = call(key_state_kernel, 16, "ww", "s", (keys, values))
    key_state, before, total = lax.optimization_barrier((key_state, before, total))
    key_parts = to_owners(key_state)
    z = before + ctx_running(total, ctx, True, F32, False)
    (query_state,) = call(query_state_kernel, 16, "wwwr", "s", (queries, keys, out_grad, z))
    key_parts, query_state = lax.optimization_barrier((key_parts, query_state))
    query_parts = to_owners(query_state)
    key_total = z_total(key_parts)
    key_base = ctx_running(key_total, ctx, True, BF16, True)
    key_running = z_running(key_parts, key_base, True)
    query_parts, key_running = lax.optimization_barrier((query_parts, key_running))
    prefix = from_owners(key_running)
    query_total = z_total(query_parts)
    query_base = ctx_running(query_total, ctx, False, BF16, True)
    spread = z_spread(where, query_parts, query_base)
    grad_queries, dfk, gv, query_sum = call(
        query_grad_kernel, 8, "wwwwra", "wffg", (queries, keys, values, out_grad, z, prefix)
    )
    sums = z_gather(query_sum)
    pieces = [spread[0]] + [None] * (group - 1)
    for d in sorted(range(1, group), key=lambda d: -min(d, group - d)):
        pairs = [(i, (i + d) % group) for i in range(group)]
        pieces[d] = lax.ppermute(spread[d], "head", pairs)
    r = ctx_running(jnp.sum(sums, axis=0), ctx, False, F32, False)
    r = r + jnp.sum(jnp.where(ranks > place, sums, 0.0), axis=0)
    grad_keys, grad_values = key_grad(where, keys, values, dfk, gv, r, pieces)
    return grad_queries, grad_keys, grad_values


def solution(mesh):
    spec = P(("ctx", "head"), None)
    body = functools.partial(shards, mesh.shape["ctx"], mesh.shape["head"])

    return jax.shard_map(
        body, mesh=mesh, in_specs=(spec,) * 4, out_specs=(spec,) * 3, check_vma=False
    )
```

```python
import functools

import jax
import jax.numpy as jnp
from jax import lax
from jax.experimental import pallas as pl
from jax.experimental.pallas import tpu as pltpu
from jax.sharding import PartitionSpec as P

HD = 128

F32 = jnp.float32
BF16 = jnp.bfloat16

LIMIT = pltpu.CompilerParams(vmem_limit_bytes=50 * 2**20)
LIMIT_LAST = pltpu.CompilerParams(vmem_limit_bytes=50 * 2**20)


def feature(real):
    return jnp.where(real > 0, real + 1.0, jnp.exp(jnp.minimum(real, 0.0)))


def dot_nn(a, b):
    return lax.dot_general(a, b, (((1,), (0,)), ((), ())), preferred_element_type=F32)


def dot_nt(a, b):
    return lax.dot_general(a, b, (((1,), (1,)), ((), ())), preferred_element_type=F32)


def dot_tn(a, b):
    return lax.dot_general(a, b, (((0,), (0,)), ((), ())), preferred_element_type=F32)


def causal(n):
    return lax.broadcasted_iota(jnp.int32, (n, n), 0) >= lax.broadcasted_iota(jnp.int32, (n, n), 1)


def columns(j):
    return slice(j * HD, (j + 1) * HD)


def head_row(ref, step, j):
    return ref[pl.ds(pl.program_id(0) * step + j, 1), :]


def put_rows(ref, step, j, row):
    at = pl.ds(pl.program_id(0) * step + j, 1)
    for member in range(ref.shape[0]):
        ref[member, at, :] = row


def each(fn, *lists):
    return [fn(*items) for items in zip(*lists)]


def key_sum_kernel(step, k_ref, sum_ref):
    for j in range(step):
        fk = feature(k_ref[:, columns(j)].astype(F32)).astype(BF16)
        put_rows(sum_ref, step, j, jnp.sum(fk.astype(F32), axis=0, keepdims=True))


def key_state_kernel(step, k_ref, v_ref, state_ref):
    heads = range(step)
    fk = [feature(k_ref[:, columns(j)].astype(F32)).astype(BF16) for j in heads]
    states = [dot_tn(fk[j], v_ref[:, columns(j)]) for j in heads]
    for j in heads:
        state_ref[j] = states[j].astype(BF16)


def scores_of(fq, fk, zrows, mask):
    scores = [jnp.where(mask, s, 0.0) for s in each(dot_nt, fq, fk)]
    dens = [
        jnp.sum(s + f.astype(F32) * zrow, axis=1, keepdims=True)
        for s, f, zrow in zip(scores, fq, zrows)
    ]
    return [s.astype(BF16) for s in scores], [1.0 / den for den in dens]


def query_state_kernel(step, q_ref, k_ref, g_ref, z_ref, state_ref):
    mask = causal(q_ref.shape[0])
    heads = range(step)
    fq = [feature(q_ref[:, columns(j)].astype(F32)).astype(BF16) for j in heads]
    fk = [feature(k_ref[:, columns(j)].astype(F32)).astype(BF16) for j in heads]
    _, inverse = scores_of(fq, fk, [head_row(z_ref, step, j) for j in heads], mask)
    dnum = [(g_ref[:, columns(j)].astype(F32) * inverse[j]).astype(BF16) for j in heads]
    states = each(dot_tn, fq, dnum)
    for j in heads:
        state_ref[j] = states[j].astype(BF16)


def num_of(fq, weights, v, s_ref):
    return [dot_nn(w, x) + dot_nn(f, s_ref[j]) for j, (f, w, x) in enumerate(zip(fq, weights, v))]


def dden_of(g_ref, num, inverse):
    shared = [
        jnp.sum(g_ref[:, columns(j)].astype(F32) * n, axis=1, keepdims=True)
        for j, n in enumerate(num)
    ]
    return [-(s * i) * i for s, i in zip(shared, inverse)]


def load_states(away, held, sems, step):
    now = pl.program_id(0)

    def load(i):
        return pltpu.make_async_copy(away.at[pl.ds(i * step, step)], held.at[i], sems.at[i])

    @pl.when(now == 0)
    def _():
        for i in range(held.shape[0]):
            load(i).start()

    def ready():
        load(now).wait()
        return held.at[now]

    return ready


def query_sum_kernel(step, q_ref, k_ref, v_ref, g_ref, z_ref, s_away, sum_ref, s_all, sems):
    ready = load_states(s_away, s_all, sems, step)
    mask = causal(q_ref.shape[0])
    heads = range(step)
    fq = [feature(q_ref[:, columns(j)].astype(F32)).astype(BF16) for j in heads]
    fk = [feature(k_ref[:, columns(j)].astype(F32)).astype(BF16) for j in heads]
    weights, inverse = scores_of(fq, fk, [head_row(z_ref, step, j) for j in heads], mask)
    num = num_of(fq, weights, [v_ref[:, columns(j)] for j in heads], ready())
    dden = dden_of(g_ref, num, inverse)
    for j in heads:
        row = jnp.sum(dden[j] * fq[j].astype(F32), axis=0, keepdims=True)
        put_rows(sum_ref, step, j, row)


def query_grad_kernel(
    step, q_ref, k_ref, v_ref, g_ref, z_ref, s_away, gq_ref, dfk_ref, gv_ref, s_all, sems
):
    ready = load_states(s_away, s_all, sems, step)
    mask = causal(q_ref.shape[0])
    heads = range(step)
    fq32 = [feature(q_ref[:, columns(j)].astype(F32)) for j in heads]
    fq = [f.astype(BF16) for f in fq32]
    fk = [feature(k_ref[:, columns(j)].astype(F32)).astype(BF16) for j in heads]
    zrows = [head_row(z_ref, step, j) for j in heads]
    v = [v_ref[:, columns(j)] for j in heads]
    weights, inverse = scores_of(fq, fk, zrows, mask)
    s_ref = ready()
    num = num_of(fq, weights, v, s_ref)
    dnum = [(g_ref[:, columns(j)].astype(F32) * inverse[j]).astype(BF16) for j in heads]
    pair = each(dot_nt, dnum, v)
    dden = dden_of(g_ref, num, inverse)
    mixing = [jnp.where(mask, p + d, 0.0).astype(BF16) for p, d in zip(pair, dden)]
    for j in heads:
        gv_ref[:, columns(j)] = dot_tn(weights[j], dnum[j])
    dfq = [
        dot_nn(mixing[j], fk[j]) + dot_nt(dnum[j], s_ref[j]) + dden[j] * zrows[j] for j in heads
    ]
    for j in heads:
        gq_ref[:, columns(j)] = (dfq[j] * jnp.minimum(fq32[j], 1.0)).astype(BF16)
    for j in heads:
        dfk_ref[:, columns(j)] = dot_tn(mixing[j], fq[j])


def key_grad_kernel(place_ref, k_hbm, v_hbm, dfk_hbm, gv_hbm, rz_ref, *refs):
    group = len(refs) - 8
    pieces, (gk_ref, gv_out_ref), loaded, sems = refs[:group], refs[group : group + 2], refs[-6:-1], refs[-1]
    rows = pieces[0].shape[0]
    owners = [lax.rem(place_ref[0] + group - d, group) for d in range(group)]
    ats = [pl.multiple_of(owner * rows, rows) for owner in owners]
    copies = [
        [
            pltpu.make_async_copy(src.at[:, pl.ds(at, rows)], dst.at[d], sems.at[n, d])
            for n, (src, dst) in enumerate(zip((k_hbm, v_hbm, dfk_hbm, gv_hbm), loaded))
        ]
        + [pltpu.make_async_copy(pieces[d], loaded[-1].at[d], sems.at[4, d])]
        for d, at in enumerate(ats)
    ]
    for some in copies:
        for copy in some:
            copy.start()
    k, v, dfk_in, gv_in, suffix = loaded
    for first in range(0, group, 2):
        work = []
        for d in (first, first + 1):
            for copy in copies[d]:
                copy.wait()
            work += [(d, j) for j in range(rows // HD)]
        states = [suffix[d, columns(j), :] for d, j in work]
        fk32 = [feature(k[d, :, columns(j)].astype(F32)) for d, j in work]
        dfk = [dot_nt(v[d, :, columns(j)], state) for (d, j), state in zip(work, states)]
        gv = [dot_nn(f.astype(BF16), state) for f, state in zip(fk32, states)]
        for f, whole, (d, j) in zip(fk32, dfk, work):
            row = rz_ref[pl.ds(owners[d] * (rows // HD) + j, 1), :]
            whole = whole + dfk_in[d, :, columns(j)] + row
            gk_ref[:, pl.ds(ats[d] + j * HD, HD)] = (whole * jnp.minimum(f, 1.0)).astype(BF16)
        for part, (d, j) in zip(gv, work):
            part = part + gv_in[d, :, columns(j)]
            gv_out_ref[:, pl.ds(ats[d] + j * HD, HD)] = part.astype(BF16)


def key_grad(place, k, v, dfk, gv, r, pieces):
    tokens, width = k.shape
    group, rows = len(pieces), pieces[0].shape[0]
    whole, away = pl.BlockSpec(memory_space=pltpu.VMEM), pl.BlockSpec(memory_space=pl.ANY)
    return pl.pallas_call(
        key_grad_kernel,
        in_specs=[pl.BlockSpec(memory_space=pltpu.SMEM)] + [away] * 4 + [whole] + [away] * group,
        out_specs=[whole] * 2,
        out_shape=[jax.ShapeDtypeStruct((tokens, width), BF16)] * 2,
        scratch_shapes=[pltpu.VMEM((group, tokens, rows), x.dtype) for x in (k, v, dfk, gv)]
        + [pltpu.VMEM((group, rows, HD), BF16), pltpu.SemaphoreType.DMA((5, group))],
        compiler_params=LIMIT_LAST,
    )(place, k, v, dfk, gv, r, *pieces)


def head_call(kernel, step, kinds_in, kinds_out, arrays, tokens, heads, group):
    wide = pl.BlockSpec((tokens, step * HD), lambda i: (0, i))
    square = pl.BlockSpec((step, HD, HD), lambda i: (i, 0, 0))
    rows = pl.BlockSpec((heads, HD), lambda i: (0, 0))
    copies = pl.BlockSpec((group, heads, HD), lambda i: (0, 0, 0))
    specs = {"a": pl.BlockSpec(memory_space=pl.ANY), "g": copies, "w": wide, "f": wide, "s": square, "r": rows}
    shapes = {
        "g": jax.ShapeDtypeStruct((group, heads, HD), F32),
        "w": jax.ShapeDtypeStruct((tokens, heads * HD), BF16),
        "f": jax.ShapeDtypeStruct((tokens, heads * HD), F32),
        "s": jax.ShapeDtypeStruct((heads, HD, HD), BF16),
        "r": jax.ShapeDtypeStruct((heads, HD), F32),
    }
    return pl.pallas_call(
        functools.partial(kernel, step),
        grid=(heads // step,),
        in_specs=[specs[t] for t in kinds_in],
        out_specs=[specs[t] for t in kinds_out],
        out_shape=[shapes[t] for t in kinds_out],
        scratch_shapes=[
            pltpu.VMEM((heads // step, step, HD, HD), BF16),
            pltpu.SemaphoreType.DMA((heads // step,)),
        ]
        if "a" in kinds_in
        else [],
        compiler_params=LIMIT if "a" in kinds_in else None,
    )(*arrays)


def z_running_kernel(forward, x_ref, base_ref, out_ref):
    n = x_ref.shape[0]
    acc = base_ref[...]
    for s in range(n):
        z = s if forward else n - 1 - s
        out_ref[z] = acc.astype(BF16)
        if s < n - 1:
            acc = acc + x_ref[z].astype(F32)


def z_total(x):
    return jnp.sum(x.astype(F32), axis=0)


def z_spread_kernel(place_ref, x_ref, base_ref, *refs):
    outs, held = refs[:-1], refs[-1]
    z_running_kernel(False, x_ref, base_ref, held)
    for d, out in enumerate(outs):
        out[...] = held[lax.rem(place_ref[0] + d, len(outs))]


def z_running(x, base, forward):
    n, rows, lanes = x.shape
    whole = pl.BlockSpec(memory_space=pltpu.VMEM)
    return pl.pallas_call(
        functools.partial(z_running_kernel, forward),
        in_specs=[whole, whole],
        out_specs=whole,
        out_shape=jax.ShapeDtypeStruct((n, rows, lanes), BF16),
    )(x, base)


def z_spread(place, x, base):
    n, rows, lanes = x.shape
    whole = pl.BlockSpec(memory_space=pltpu.VMEM)
    return pl.pallas_call(
        z_spread_kernel,
        in_specs=[pl.BlockSpec(memory_space=pltpu.SMEM), whole, whole],
        out_specs=[whole] * n,
        out_shape=[jax.ShapeDtypeStruct((rows, lanes), BF16)] * n,
        scratch_shapes=[pltpu.VMEM((n, rows, lanes), BF16)],
    )(place, x, base)


def level(value, n, place, hop, forward, wire, need_total):
    sent = value.astype(wire)
    got = [hop(sent, d, need_total).astype(F32) for d in range(1, n)]
    if not need_total:
        return sum(got[1:], got[0]), None
    before = sum(
        jnp.where((place >= d) if forward else (place < n - d), g, 0.0) for d, g in enumerate(got, 1)
    )
    return before, sum(got, value)


def grid_of(ctx):
    side = 1
    while side * side * 2 < ctx:
        side += 1
    return side


def ctx_hop(side, which, forward):
    def hop(value, d, wrap):
        d = d if forward else -d
        pairs = []
        for x in range(side):
            for y in range(side):
                to = (x, y + d) if which == "y" else (x + d, y)
                if not wrap and not all(0 <= t < side for t in to):
                    continue
                at = (to[0] % side) * side + to[1] % side
                pairs += [((x * side + y) * 2 + c, at * 2 + c) for c in range(2)]
        return lax.ppermute(value, "ctx", pairs)

    return hop


def swap_cores(value, ctx):
    return lax.ppermute(value, "ctx", [(i, i ^ 1) for i in range(ctx)])


def ctx_running(total, ctx, forward, wire, split):
    side = grid_of(ctx)
    place = lax.axis_index("ctx")
    core, y, x = place % 2, (place // 2) % side, place // (2 * side)
    other = swap_cores(total, ctx)
    by_core = jnp.where((core == 1) if forward else (core == 0), other, 0.0)
    chip = total + other
    half = total.shape[0] // 2
    if split:
        chip = jnp.where(core == 0, chip[:half], chip[half:])
    by_y, row = level(chip, side, y, ctx_hop(side, "y", forward), forward, wire, True)
    by_x, _ = level(row, side, x, ctx_hop(side, "x", forward), forward, wire, False)
    base = by_y + by_x
    if split:
        got = swap_cores(base, ctx)
        base = jnp.concatenate([jnp.where(core == 0, base, got), jnp.where(core == 0, got, base)])
    return by_core + base


def z_gather(copies):
    return lax.all_to_all(copies, "head", 0, 0, tiled=True)


def shards(ctx, group, queries, keys, values, out_grad):
    tokens, width = queries.shape
    heads = width // HD
    call = functools.partial(head_call, tokens=tokens, heads=heads, group=group)
    owned = heads * HD // group
    place = lax.axis_index("head")

    def to_owners(state):
        return lax.all_to_all(state.reshape(group, owned, HD), "head", 0, 0, tiled=True)

    def from_owners(x):
        return lax.all_to_all(x, "head", 0, 0, tiled=True).reshape(heads, HD, HD)

    ranks = jnp.arange(group)[:, None, None]
    where = jnp.full((1,), place, jnp.int32)
    (key_sum,) = call(key_sum_kernel, 16, "w", "g", (keys,))
    sums = z_gather(key_sum)
    before = jnp.sum(jnp.where(ranks < place, sums, 0.0), axis=0)
    total = jnp.sum(sums, axis=0)
    (key_state,) = call(key_state_kernel, 16, "ww", "s", (keys, values))
    key_state, before, total = lax.optimization_barrier((key_state, before, total))
    key_parts = to_owners(key_state)
    z = before + ctx_running(total, ctx, True, F32, False)
    (query_state,) = call(query_state_kernel, 16, "wwwr", "s", (queries, keys, out_grad, z))
    key_parts, query_state = lax.optimization_barrier((key_parts, query_state))
    query_parts = to_owners(query_state)
    key_total = z_total(key_parts)
    key_base = ctx_running(key_total, ctx, True, BF16, True)
    key_running = z_running(key_parts, key_base, True)
    query_parts, key_running = lax.optimization_barrier((query_parts, key_running))
    prefix = from_owners(key_running)
    query_total = z_total(query_parts)
    query_base = ctx_running(query_total, ctx, False, BF16, True)
    spread = z_spread(where, query_parts, query_base)
    locals_in = (queries, keys, values, out_grad, z, prefix)
    (query_sum,) = call(query_sum_kernel, 16, "wwwwra", "g", locals_in)
    sums = z_gather(query_sum)
    grad_queries, dfk, gv = call(query_grad_kernel, 8, "wwwwra", "wff", locals_in)
    pieces = [spread[0]] + [None] * (group - 1)
    for d in sorted(range(1, group), key=lambda d: -min(d, group - d)):
        pairs = [(i, (i + d) % group) for i in range(group)]
        pieces[d] = lax.ppermute(spread[d], "head", pairs)
    r = ctx_running(jnp.sum(sums, axis=0), ctx, False, F32, False)
    r = r + jnp.sum(jnp.where(ranks > place, sums, 0.0), axis=0)
    grad_keys, grad_values = key_grad(where, keys, values, dfk, gv, r, pieces)
    return grad_queries, grad_keys, grad_values


def solution(mesh):
    spec = P(("ctx", "head"), None)
    body = functools.partial(shards, mesh.shape["ctx"], mesh.shape["head"])

    return jax.shard_map(
        body, mesh=mesh, in_specs=(spec,) * 4, out_specs=(spec,) * 3, check_vma=False
    )
```
